32 devices in a mesh: gx: 4 (over y, x), gy: 8 (over z, core).
Axes of the slice: x: 2, y: 2, z: 4, core: 2. Of those that a mesh axis runs over, the one named last changes fastest.
Arguments:
- background: bfloat16 [40, 64, 256, 128], P(None, 'gx', 'gy'), may hold values from -6 to 6
- obs_perturb: bfloat16 [4, 8, 40, 256], P('gx', 'gy'), may hold values from -1.796875 to 1.796875
- innovation: float32 [4, 8, 256], P('gx', 'gy'), may hold values from -3.8 to 3.8
- obs_precision: float32 [4, 8, 256], P('gx', 'gy'), may hold values from 0.3 to 3
- obs_column: int32 [4, 8, 256], P('gx', 'gy'), may hold values from 0 to 511
- obs_count: int32 [4, 8], P('gx', 'gy'), may hold values from 64 to 256, as said below
Outputs:
- analysis: bfloat16 [40, 64, 256, 128], P(None, 'gx', 'gy')
The draws below stay inside these ranges and needn't reach their ends.
Inputs may be any that keep to these rules, and one draw needn't show every extreme that they name: Slots 0 to obs_count - 1 of a tile hold observations, the others are padding; in every draw some tile has all 256 slots live.
All inputs are finite; a program needn't handle non-finite values.
Results may differ from the reference program's by a relative error of at most 0.001.
Values sent between devices are 32-bit elements; how exact they have to be, the bound alone decides.
No kernel may reach another device: no remote copies, remote signals or barrier semaphores. Data moves between devices by JAX's collectives and lax.ppermute only.
A program may use at most 128 MiB of HBM per device.

```python
import math
import jax
import jax.numpy as jnp
from jax import lax

MEMBERS = 40
LEV = 128
OBS_SLOTS_TILE = 256
RX = 8
RY = 16
SPAN = 2
TILES_X = 4
TILES_Y = 8
CX = 16
CY = 32
NX = 64
NY = 256
N_GX = 4
N_GY = 8


def draw_innovation(key, part):
    extent = (TILES_X, TILES_Y, OBS_SLOTS_TILE)
    rising = 1.0 + 2.0 * jnp.arange(TILES_Y, dtype=jnp.float32) / (TILES_Y - 1)
    jitter = jnp.clip(jax.random.normal(key, extent, jnp.float32), -4.0, 4.0)
    tilted = jnp.ones((TILES_X,), jnp.float32)
    return 0.3 * rising[None, :, None] * tilted[:, None, None] * jitter


def draw_obs_count(key, part):
    counts = jax.random.randint(jax.random.fold_in(key, 11), (TILES_X, TILES_Y), OBS_SLOTS_TILE // 4, OBS_SLOTS_TILE + 1)
    selected_entry = jax.random.randint(jax.random.fold_in(key, 12), (), 0, TILES_X * TILES_Y)
    places = jnp.arange(TILES_X * TILES_Y).reshape(TILES_X, TILES_Y)
    return jnp.where(places == selected_entry, OBS_SLOTS_TILE, counts).astype(jnp.int32)


def place_ends(values, key, low, largest):
    shape = values.shape
    place = [jax.random.randint(jax.random.fold_in(key, axis), (), 0, shape[axis]) for axis in range(len(shape))]
    values = values.at[tuple(place)].set(low)
    longest = shape.index(max(shape))
    place[longest] = (place[longest] + 1) % shape[longest]
    return values.at[tuple(place)].set(largest)


def block_levels(own_key, shape, shards, least, largest):
    level, own = 1.0, jax.random.fold_in(own_key, 6)
    for dim, parts in shards:
        draws = jnp.exp(jax.random.uniform(jax.random.fold_in(own, dim), (parts,), jnp.float32, least / len(shards), largest / len(shards)))
        level = level * jnp.repeat(draws, shape[dim] // parts).reshape([-1 if axis == dim else 1 for axis in range(len(shape))])
    return level


def centred(rng, shape, scale, most, shards=(), kind=jnp.bfloat16):
    drawn = scale * jax.random.normal(rng, shape, jnp.float32)
    if shards:
        drawn = drawn * block_levels(rng, shape, shards, -0.22, 0.18)
    return jnp.clip(drawn, -most, most).astype(kind)


def setup_inputs(seed: int = 0) -> dict:
    key_list = jax.random.split(jax.random.key(seed), 7)
    background = centred(key_list[0], (MEMBERS, NX, NY, LEV), 1.0, 6.0, ((1, 4), (2, 8)))
    obs_perturb = centred(key_list[1], (TILES_X, TILES_Y, MEMBERS, OBS_SLOTS_TILE), 0.3, 1.796875, ((0, 4), (1, 8)))
    innovation = draw_innovation(jax.random.fold_in(key_list[6], 71), 0)
    obs_precision = jnp.clip(jnp.exp(math.log(3.0) - 2.3025851 * jax.random.uniform(key_list[3], (TILES_X, TILES_Y, OBS_SLOTS_TILE), jnp.float32) ** block_levels(key_list[3], (TILES_X, TILES_Y, OBS_SLOTS_TILE), ((0, 4), (1, 8)), -0.2, 0.2)), 0.3, 3.0)
    obs_column = place_ends(jax.random.randint(key_list[4], (TILES_X, TILES_Y, OBS_SLOTS_TILE), 0, CX * CY), jax.random.fold_in(key_list[4], 1), 0, (CX * CY) - 1).astype(jnp.int32)
    obs_count = draw_obs_count(jax.random.fold_in(key_list[6], 71), 0)
    return {"background": background, "obs_perturb": obs_perturb, "innovation": innovation, "obs_precision": obs_precision, "obs_column": obs_column, "obs_count": obs_count}


def pair_table(centered, values):
    members = centered.shape[0]
    squares = (centered[:, None, :] * centered[None, :, :]).reshape(members * members, centered.shape[1])
    return jnp.concatenate([squares, centered * values[None, :]], axis=0)

def taper(east_pos, north_pos, centre_east, centre_north, period, radius):
    offset_east = jnp.mod(east_pos[:, None] - centre_east[None, :] + 0.5 * period, period) - 0.5 * period
    offset_north = north_pos[:, None] - centre_north[None, :]
    ratio = (offset_east * offset_east + offset_north * offset_north) / (radius * radius)
    return jnp.square(jnp.maximum(1.0 - ratio, 0.0))

def region_centres(tile_east, northward_tile, count_east, count_north, span, width_east, width_north):
    rows_east = (jnp.arange(count_east) * span).astype(jnp.float32) + 0.5 * span
    rows_north = (jnp.arange(count_north) * span).astype(jnp.float32) + 0.5 * span
    base_east = (tile_east * width_east).astype(jnp.float32)
    base_north = (northward_tile * width_north).astype(jnp.float32)
    centre_east = jnp.broadcast_to(base_east + rows_east[:, None], (count_east, count_north)).reshape(-1)
    centre_north = jnp.broadcast_to(base_north + rows_north[None, :], (count_east, count_north)).reshape(-1)
    return (centre_east, centre_north)

def chol_lower(system):
    members = system.shape[0]
    rows = jnp.arange(members)
    remain = system
    columns = []
    for pivot_id in range(members):
        pivot = jnp.sqrt(remain[pivot_id, pivot_id])
        column = jnp.where((rows >= pivot_id)[:, None], remain[:, pivot_id] / pivot[None, :], 0.0)
        columns.append(column)
        remain = remain - column[:, None, :] * column[None, :, :]
    return jnp.stack(columns, axis=1)

def lower_inverse(factor):
    members = factor.shape[0]
    remain = jnp.broadcast_to(jnp.eye(members, dtype=factor.dtype)[:, :, None], factor.shape)
    solved = []
    for pivot_id in range(members):
        row_now = remain[pivot_id] / factor[pivot_id, pivot_id][None, :]
        solved.append(row_now)
        remain = remain - factor[:, pivot_id][:, None, :] * row_now[None, :, :]
    return jnp.stack(solved, axis=0)

def transform_of(gram, prior_term, members):
    square = members * members
    system = gram[:square].reshape(members, members, -1) + prior_term * jnp.eye(members, dtype=gram.dtype)[:, :, None]
    pull = gram[square:]
    inverse = lower_inverse(chol_lower(system))
    inner = jnp.einsum('imr,mr->ir', inverse, pull, precision=lax.Precision.HIGHEST)
    mean_weights = jnp.einsum('imr,ir->mr', inverse, inner, precision=lax.Precision.HIGHEST)
    return mean_weights[:, None, :] + math.sqrt(members - 1) * jnp.transpose(inverse, (1, 0, 2))

def interp_matrix(columns, regions, span):
    position = jnp.arange(columns).astype(jnp.float32) + 0.5
    centre = (jnp.arange(regions + 2) - 1).astype(jnp.float32) * span + 0.5 * span
    return jnp.maximum(1.0 - jnp.abs(position[:, None] - centre[None, :]) / span, 0.0)

def apply_tile(state_tile, local_frame, span):
    members, cols_east, cols_north, levels = state_tile.shape
    interpolation_rows = interp_matrix(cols_east, local_frame.shape[0] - 2, span)
    interp_cols = interp_matrix(cols_north, local_frame.shape[1] - 2, span)
    halfway_result = jnp.einsum('br,rjg->bjg', interpolation_rows, local_frame, precision=lax.Precision.HIGHEST)
    column_transform = jnp.einsum('bq,aqm->abm', interp_cols, halfway_result, precision=lax.Precision.HIGHEST)
    column_transform = column_transform.reshape(cols_east, cols_north, members, members)
    float_state = state_tile.astype(jnp.float32)
    centre_mean = lax.optimization_barrier(jnp.mean(float_state, axis=0))
    spread = float_state - centre_mean[None]
    update = jnp.einsum('jabl,abjk->kabl', spread, column_transform, precision=lax.Precision.HIGHEST)
    return (centre_mean[None] + update).astype(jnp.bfloat16)

def reference(background, obs_perturb, innovation, obs_precision, obs_column, obs_count):
    members = MEMBERS
    square = members * members
    centered = obs_perturb.astype(jnp.float32)
    centered = centered - lax.optimization_barrier(jnp.mean(centered, axis=2, keepdims=True))
    slots = jnp.arange(OBS_SLOTS_TILE, dtype=jnp.int32)
    live = (slots[None, None, :] < obs_count[:, :, None]).astype(jnp.float32)
    weight = obs_precision * live
    tiles_east = jnp.arange(N_GX, dtype=jnp.int32)[:, None, None]
    tiles_north = jnp.arange(N_GY, dtype=jnp.int32)[None, :, None]
    east_pos = (tiles_east * CX + obs_column // CY).astype(jnp.float32) + 0.5
    north_pos = (tiles_north * CY + obs_column % CY).astype(jnp.float32) + 0.5
    numer = jnp.sum(weight * innovation * innovation)
    denom = jnp.sum(weight * lax.optimization_barrier(jnp.sum(centered * centered, axis=2))) / (members - 1)
    prior_term = (members - 1) / (numer / denom)
    period = float(NX)
    radius = float(CX)
    zero = jnp.zeros((), jnp.int32)

    def tile_weight_matrix(tile_id):
        tile_east = tile_id // N_GY
        northward_tile = tile_id % N_GY
        centre_east, centre_north = region_centres(tile_east, northward_tile, RX, RY, SPAN, CX, CY)
        gram = jnp.zeros((square + members, RX * RY), jnp.float32)
        for step_east in (-1, 0, 1):
            for step_north in (-1, 0, 1):
                source_east = (tile_east + step_east) % N_GX
                source_north = (northward_tile + step_north) % N_GY
                products = pair_table(centered[source_east, source_north], innovation[source_east, source_north])
                reach = taper(east_pos[source_east, source_north], north_pos[source_east, source_north], centre_east, centre_north, period, radius)
                reach = reach * weight[source_east, source_north][:, None]
                gram = gram + jnp.dot(products, reach, precision=lax.Precision.HIGHEST, preferred_element_type=jnp.float32)
        trans = transform_of(gram, prior_term, members)
        return jnp.transpose(trans, (2, 0, 1)).reshape(RX, RY, square)
    tile_ids = jnp.arange(N_GX * N_GY, dtype=jnp.int32)
    grids = lax.map(tile_weight_matrix, tile_ids)
    grids = grids.reshape(N_GX, N_GY, RX, RY, square).transpose(0, 2, 1, 3, 4).reshape(N_GX * RX, N_GY * RY, square)
    padded = jnp.pad(grids, ((1, 1), (0, 0), (0, 0)), mode='wrap')
    padded = jnp.pad(padded, ((0, 0), (1, 1), (0, 0)), mode='edge')

    def tile_state(tile_id):
        tile_east = tile_id // N_GY
        northward_tile = tile_id % N_GY
        local_frame = lax.dynamic_slice(padded, ((tile_east * RX).astype(jnp.int32), (northward_tile * RY).astype(jnp.int32), zero), (RX + 2, RY + 2, square))
        state_tile = lax.dynamic_slice(background, (zero, (tile_east * CX).astype(jnp.int32), (northward_tile * CY).astype(jnp.int32), zero), (members, CX, CY, LEV))
        return apply_tile(state_tile, local_frame, float(SPAN))
    results = lax.map(tile_state, tile_ids)
    results = results.reshape(N_GX, N_GY, members, CX, CY, LEV).transpose(2, 0, 3, 1, 4, 5)
    return results.reshape(members, NX, NY, LEV)
```

```python
import functools
import math

import jax
import jax.numpy as jnp
from jax import lax
from jax.experimental import pallas as pl
from jax.experimental.pallas import tpu as pltpu
from jax.sharding import PartitionSpec as P

SPAN = 2
LANES = 128
SUB = 8
ROWS = 48
F32 = jnp.float32
BF16 = jnp.bfloat16


def pair_rows(members):
    offsets, total = [], 0
    for i in range(members):
        offsets.append(total)
        total += members - (i // SUB) * SUB
    pull = total
    total += members
    return offsets, pull, -(-total // 16) * 16


def prep_kernel(cols_east, cols_north, count_ref, perturb_ref, innov_ref, prec_ref, column_ref, out_ref):
    members, slots = perturb_ref.shape
    tile_east, tile_north = lax.axis_index("gx"), lax.axis_index("gy")
    spread = perturb_ref[...].astype(F32)
    spread = spread - jnp.sum(spread, axis=0, keepdims=True) / members
    lane = lax.broadcasted_iota(jnp.int32, (1, slots), 1)
    weight = jnp.where(lane < count_ref[0, 0], prec_ref[...], 0.0)
    root = jnp.sqrt(weight)
    values = innov_ref[...]
    column = column_ref[...]
    east = lax.div(column, cols_north)
    north = column - east * cols_north
    east = (tile_east * cols_east + east).astype(F32) + 0.5
    north = (tile_north * cols_north + north).astype(F32) + 0.5
    numer = jnp.sum(weight * values * values, axis=1, keepdims=True)
    variance = jnp.sum(spread * spread, axis=0, keepdims=True)
    denom = jnp.sum(weight * variance, axis=1, keepdims=True) / (members - 1)
    out_ref[0:members, :] = spread * root
    row = lax.broadcasted_iota(jnp.int32, (ROWS - members, slots), 0)
    rest = jnp.zeros((ROWS - members, slots), F32)
    for place, value in enumerate((values * root, east, north, numer, denom)):
        rest = jnp.where(row == place, value, rest)
    out_ref[members:ROWS, :] = rest


def gram_kernel(members, cols_east, cols_north, obs_ref, out_ref, lhs_hi, lhs_lo, rhs_hi, rhs_lo):
    tiles = obs_ref.shape[0] // ROWS
    slots = obs_ref.shape[1]
    offsets, pull_row, total = pair_rows(members)
    regions_north = cols_north // SPAN
    deep = regions_north // 2 + 2
    lanes = 2 * LANES
    tile_east, tile_north = lax.axis_index("gx"), lax.axis_index("gy")
    count_north = lax.axis_size("gy")
    lane = lax.broadcasted_iota(jnp.int32, (1, lanes), 1)
    half = (lane >= LANES).astype(jnp.int32)
    inner = (lane - half * LANES).astype(F32)
    place_east = jnp.floor((inner + 0.5) / deep)
    place_north = inner - place_east * deep
    centre_east = (tile_east * cols_east).astype(F32) + (place_east - 1.0) * SPAN + 0.5 * SPAN
    place_north = place_north + (tile_north * regions_north + half * (regions_north // 2) - 1).astype(F32)
    place_north = jnp.clip(place_north, 0.0, float(count_north * regions_north - 1))
    centre_north = place_north * SPAN + 0.5 * SPAN
    period = float(lax.axis_size("gx") * cols_east)
    radius = float(cols_east)
    for t in range(tiles):
        base = t * ROWS
        place = jnp.transpose(obs_ref[base + members : base + ROWS, :])
        east, north = place[:, 1:2], place[:, 2:3]
        ahead = east - centre_east + 0.5 * period
        away = ahead - period * jnp.floor(ahead * (1.0 / period)) - 0.5 * period
        up = north - centre_north
        near = jnp.maximum(1.0 - (away * away + up * up) * (1.0 / (radius * radius)), 0.0)
        taper = near * near
        hi = taper.astype(BF16)
        rhs_hi[t * slots : (t + 1) * slots, :] = hi
        rhs_lo[t * slots : (t + 1) * slots, :] = (taper - hi.astype(F32)).astype(BF16)
        span = slice(t * slots, (t + 1) * slots)
        for i in range(0, members, 2):
            first = (i // SUB) * SUB
            rows = obs_ref[base + first : base + members, :]
            table = jnp.concatenate(
                [obs_ref[base + i : base + i + 1, :] * rows, obs_ref[base + i + 1 : base + i + 2, :] * rows], axis=0
            )
            hi = table.astype(BF16)
            lhs_hi[offsets[i] : offsets[i] + table.shape[0], span] = hi
            lhs_lo[offsets[i] : offsets[i] + table.shape[0], span] = (table - hi.astype(F32)).astype(BF16)
        table = obs_ref[base + members : base + members + 1, :] * obs_ref[base : base + members, :]
        table = jnp.concatenate([table, jnp.zeros((total - pull_row - members, slots), F32)], axis=0)
        hi = table.astype(BF16)
        lhs_hi[pull_row:total, span] = hi
        lhs_lo[pull_row:total, span] = (table - hi.astype(F32)).astype(BF16)
    left = jnp.concatenate([lhs_hi[...], lhs_lo[...], lhs_hi[...]], axis=1)
    right = jnp.concatenate([rhs_hi[...], rhs_hi[...], rhs_lo[...]], axis=0)
    out_ref[...] = jnp.dot(left, right, preferred_element_type=F32)


def gram_table(bundles, members, cols_east, cols_north):
    total = pair_rows(members)[2]
    deep = bundles.shape[0] // ROWS * bundles.shape[1]
    return pl.pallas_call(
        functools.partial(gram_kernel, members, cols_east, cols_north),
        out_shape=jax.ShapeDtypeStruct((total, 2 * LANES), F32),
        in_specs=[pl.BlockSpec(memory_space=pltpu.VMEM)],
        out_specs=pl.BlockSpec(memory_space=pltpu.VMEM),
        scratch_shapes=[
            pltpu.VMEM((total, deep), BF16),
            pltpu.VMEM((total, deep), BF16),
            pltpu.VMEM((deep, 2 * LANES), BF16),
            pltpu.VMEM((deep, 2 * LANES), BF16),
        ],
        compiler_params=pltpu.CompilerParams(vmem_limit_bytes=24 << 20),
        cost_estimate=pl.CostEstimate(flops=6 * total * deep * 2 * LANES, bytes_accessed=1 << 21, transcendentals=0),
        name="gram_table",
    )(bundles)


def analysis_kernel(
    members, grams, sums_a, sums_b, state_ref, out_ref, u_ref, v_ref, t_ref, s_ref, w_ref, b_ref, o_ref,
    state_v, out_v, in_sem, out_sem,
):
    _, cols_east, cols_north, levels = state_v.shape
    offsets, pull_row, _ = pair_rows(members)
    wide = 2 * LANES
    blocks = members // SUB
    pitch = s_ref.shape[0] // members
    pitch_b = b_ref.shape[0] // members
    half_cols = cols_north // 2
    half = cols_east * half_cols
    deep = half_cols // SPAN + 2

    def fetch(a):
        return pltpu.make_async_copy(state_ref.at[:, a], state_v.at[:, a], in_sem.at[a])

    def flush(a):
        return pltpu.make_async_copy(out_v.at[:, a], out_ref.at[:, a], out_sem.at[a])

    for a in range(cols_east):
        fetch(a).start()

    row = lax.broadcasted_iota(jnp.int32, (half, LANES), 0).astype(F32)
    lane = lax.broadcasted_iota(jnp.int32, (half, LANES), 1).astype(F32)
    col_east = jnp.floor((row + 0.5) / half_cols)
    col_north = row - col_east * half_cols
    reg_east = jnp.floor((lane + 0.5) / deep)
    reg_north = lane - reg_east * deep
    hat_east = jnp.maximum(1.0 - jnp.abs(col_east + 0.5 - ((reg_east - 1.0) * SPAN + 0.5 * SPAN)) / SPAN, 0.0)
    hat_north = jnp.maximum(1.0 - jnp.abs(col_north + 0.5 - ((reg_north - 1.0) * SPAN + 0.5 * SPAN)) / SPAN, 0.0)
    hats = (hat_east * hat_north).astype(BF16)
    w_ref[:, 0:LANES] = hats
    w_ref[:, LANES:wide] = hats

    total = sums_a[...] + sums_b[...]
    prior = (members - 1) / (total[0:1, 0:1] / total[1:2, 0:1])

    sub = lax.broadcasted_iota(jnp.int32, (SUB, wide), 0)

    def gram(row0):
        return functools.reduce(lambda x, y: x + y, [g[row0 : row0 + SUB, :] for g in grams])

    pulls = [gram(pull_row + SUB * b) for b in range(blocks)]
    mean_w = [jnp.zeros((SUB, wide), F32) for _ in range(blocks)]
    row_sums = []
    for i in range(members):
        own = i // SUB
        acc_u = [gram(offsets[i] + SUB * b) for b in range(blocks - own)]
        at = sub == i % SUB
        acc_u[0] = acc_u[0] + jnp.where(at, prior, 0.0)
        acc_v = [jnp.zeros((SUB, wide), F32) for _ in range(own)] + [jnp.where(at, 1.0, 0.0)]
        for p in range(i):
            factor = u_ref[p * members + i : p * members + i + 1, :]
            for b in range(own, blocks):
                acc_u[b - own] = acc_u[b - own] - factor * u_ref[p * members + SUB * b : p * members + SUB * (b + 1), :]
            for b in range(p // SUB + 1):
                acc_v[b] = acc_v[b] - factor * v_ref[p * members + SUB * b : p * members + SUB * (b + 1), :]
        inv = lax.rsqrt(acc_u[0][i % SUB : i % SUB + 1, :])
        for b in range(own, blocks):
            u_ref[i * members + SUB * b : i * members + SUB * (b + 1), :] = acc_u[b - own] * inv
        solved, whole = None, None
        acc_v = [x * inv for x in acc_v]
        for b in range(own + 1):
            v_ref[i * members + SUB * b : i * members + SUB * (b + 1), :] = acc_v[b]
            part = acc_v[b] * pulls[b]
            solved = part if solved is None else solved + part
            whole = acc_v[b] if whole is None else whole + acc_v[b]
        solved = jnp.sum(solved, axis=0, keepdims=True)
        row_sums.append(jnp.sum(whole, axis=0, keepdims=True))
        for b in range(own + 1):
            mean_w[b] = mean_w[b] + solved * acc_v[b]

    scale = math.sqrt(members - 1)
    mean_sum = jnp.sum(functools.reduce(lambda x, y: x + y, mean_w), axis=0, keepdims=True)
    for k in range(members):
        own = k // SUB
        shift = (1.0 - mean_sum - scale * row_sums[k]) * (1.0 / members)
        parts = []
        for b in range(blocks):
            x = mean_w[b] + shift
            if b <= own:
                x = x + scale * v_ref[k * members + SUB * b : k * members + SUB * (b + 1), :]
            parts.append(x)
        parts.append(jnp.zeros((ROWS - members, wide), F32))
        table = jnp.concatenate(parts, axis=0)
        hi = table.astype(BF16)
        lo = (table - hi.astype(F32)).astype(BF16)
        for h in range(2):
            t_ref[h, k * ROWS : (k + 1) * ROWS, 0:LANES] = hi[:, h * LANES : (h + 1) * LANES]
            t_ref[h, k * ROWS : (k + 1) * ROWS, LANES:wide] = lo[:, h * LANES : (h + 1) * LANES]

    gap = jnp.zeros((LANES - 2 * ROWS, wide), BF16)
    for h in range(2):
        for k in range(0, members, 2):
            first = t_ref[h, k * ROWS : (k + 1) * ROWS, :]
            second = t_ref[h, (k + 1) * ROWS : (k + 2) * ROWS, :]
            right = jnp.concatenate([first, first, gap, second, second, gap], axis=0)
            both = lax.dot_general(w_ref[...], right, (((1,), (1,)), ((), ())), preferred_element_type=F32)
            s_ref[k * pitch + h * half : k * pitch + (h + 1) * half, :] = both[:, 0:LANES]
            s_ref[(k + 1) * pitch + h * half : (k + 1) * pitch + (h + 1) * half, :] = both[:, LANES:wide]

    low_lane = lax.broadcasted_iota(jnp.int32, (members, LANES), 1) >= ROWS
    gap_a = jnp.zeros((ROWS - members, levels), BF16)
    gap_b = jnp.zeros((LANES - 2 * ROWS, levels), BF16)

    def column_row(a, carry):
        fetch(a).wait()
        for j in range(members):
            b_ref[j * pitch_b : j * pitch_b + cols_north, :] = state_v[j, a].astype(F32)
        for b in range(cols_north):
            h, within = b // half_cols, b % half_cols
            left = s_ref[pl.ds(h * half + a * half_cols + within, members, stride=pitch), :]
            high = left.astype(BF16).astype(F32)
            left = jnp.where(low_lane, left - high, left).astype(BF16)
            column = b_ref[pl.ds(b, members, stride=pitch_b), :].astype(BF16)
            right = jnp.concatenate([column, gap_a, column, gap_a, gap_b], axis=0)
            o_ref[b * members : (b + 1) * members, :] = jnp.dot(left, right, preferred_element_type=F32)
        for k in range(members):
            out_v[k, a] = o_ref[pl.ds(k, cols_north, stride=members), :].astype(BF16)
        flush(a).start()
        return carry

    lax.fori_loop(0, cols_east, column_row, 0)
    for a in range(cols_east):
        flush(a).wait()


def analyse(grams, sums_a, sums_b, background):
    members, cols_east, cols_north, levels = background.shape
    columns = cols_east * cols_north
    count = len(grams)

    def body(*refs):
        analysis_kernel(members, refs[:count], *refs[count:])

    vmem = pl.BlockSpec(memory_space=pltpu.VMEM)
    hbm = pl.BlockSpec(memory_space=pl.ANY)
    pitch = columns + SUB
    return pl.pallas_call(
        body,
        out_shape=jax.ShapeDtypeStruct(background.shape, BF16),
        in_specs=[vmem] * (count + 2) + [hbm],
        out_specs=hbm,
        scratch_shapes=[
            pltpu.VMEM((members * members, 2 * LANES), F32),
            pltpu.VMEM((members * members, 2 * LANES), F32),
            pltpu.VMEM((2, members * ROWS, 2 * LANES), BF16),
            pltpu.VMEM((members * pitch, LANES), F32),
            pltpu.VMEM((columns // 2, 2 * LANES), BF16),
            pltpu.VMEM((members * (cols_north + SUB), levels), F32),
            pltpu.VMEM((cols_north * members, levels), F32),
            pltpu.VMEM(background.shape, BF16),
            pltpu.VMEM(background.shape, BF16),
            pltpu.SemaphoreType.DMA((cols_east,)),
            pltpu.SemaphoreType.DMA((cols_east,)),
        ],
        compiler_params=pltpu.CompilerParams(vmem_limit_bytes=48 << 20),
        name="analyse",
    )(*grams, sums_a, sums_b, background)


def rotate(value, axis, step):
    count = lax.axis_size(axis)
    return lax.ppermute(value, axis, [(i, (i + step) % count) for i in range(count)])


def slide(value, axis, step):
    count = lax.axis_size(axis)
    return lax.ppermute(value, axis, [(i, i + step) for i in range(count) if 0 <= i + step < count])


def swap(value, axis, bit):
    count = lax.axis_size(axis)
    return lax.ppermute(value, axis, [(i, i ^ bit) for i in range(count)])


def per_device(background, obs_perturb, innovation, obs_precision, obs_column, obs_count):
    members, cols_east, cols_north, levels = background.shape
    slots = obs_perturb.shape[3]
    count_east, count_north = lax.axis_size("gx"), lax.axis_size("gy")
    vmem = pl.BlockSpec(memory_space=pltpu.VMEM)
    bundle = pl.pallas_call(
        functools.partial(prep_kernel, cols_east, cols_north),
        out_shape=jax.ShapeDtypeStruct((ROWS, slots), F32),
        in_specs=[pl.BlockSpec(memory_space=pltpu.SMEM)] + [vmem] * 4,
        out_specs=vmem,
        name="prep",
    )(obs_count, obs_perturb[0, 0], innovation[0], obs_precision[0], obs_column[0])
    steps = sorted({s % count_east for s in (-2, -1, 1, 2)} - {0})
    own = jnp.concatenate([bundle] + [rotate(bundle, "gx", s) for s in steps], axis=0)
    below = slide(own, "gy", 1)
    above = slide(own, "gy", -1)

    def row_sum(bundles):
        each = bundles.reshape(-1, ROWS, slots)[:, members + 3 : members + 5, 0:LANES]
        return jnp.sum(each, axis=0)

    if len(steps) + 1 == count_east and count_north & (count_north - 1) == 0 and count_north >= 4:
        north = lax.axis_index("gy")
        beside = jnp.where(north % 2 == 0, row_sum(above), row_sum(below))
        total = row_sum(own) + beside
        bit = 2
        while 2 * bit < count_north:
            total = total + swap(total, "gy", bit)
            bit *= 2
        other = swap(total, "gy", bit)
    else:
        total = lax.psum(bundle[members + 3 : members + 5, 0:LANES], ("gx", "gy"))
        other = jnp.zeros_like(total)
    grams = [gram_table(x, members, cols_east, cols_north) for x in (own, below, above)]
    return analyse(grams, total, other, background)


def solution(mesh):
    return jax.shard_map(
        per_device,
        mesh=mesh,
        in_specs=(
            P(None, "gx", "gy", None),
            P("gx", "gy", None, None),
            P("gx", "gy", None),
            P("gx", "gy", None),
            P("gx", "gy", None),
            P("gx", "gy"),
        ),
        out_specs=P(None, "gx", "gy", None),
        check_vma=False,
    )
```

```python
import functools
import math

import jax
import jax.numpy as jnp
from jax import lax
from jax.experimental import pallas as pl
from jax.experimental.pallas import tpu as pltpu
from jax.sharding import PartitionSpec as P

SPAN = 2
LANES = 128
SUB = 8
ROWS = 48
SLOT = 64
F32 = jnp.float32
BF16 = jnp.bfloat16


def pair_rows(members):
    offsets, total = [], 0
    for i in range(members):
        offsets.append(total)
        total += members - (i // SUB) * SUB
    pull = total
    total += members
    return offsets, pull, -(-total // 16) * 16


def prep_kernel(
    cols_east, cols_north, count_ref, perturb_hbm, innov_hbm, prec_hbm, column_hbm, out_ref,
    perturb_ref, innov_ref, prec_ref, column_ref, sem,
):
    pairs = ((perturb_hbm, perturb_ref), (innov_hbm, innov_ref), (prec_hbm, prec_ref), (column_hbm, column_ref))
    copies = [pltpu.make_async_copy(src, dst, sem.at[n]) for n, (src, dst) in enumerate(pairs)]
    for copy in copies:
        copy.start()
    for copy in copies:
        copy.wait()
    members, slots = perturb_ref.shape
    tile_east, tile_north = lax.axis_index("gx"), lax.axis_index("gy")
    values, column = innov_ref[...], column_ref[...].astype(F32)
    spread = perturb_ref[...].astype(F32)
    spread = spread - jnp.sum(spread, axis=0, keepdims=True) / members
    lane = lax.broadcasted_iota(jnp.int32, (1, slots), 1)
    weight = jnp.where(lane < count_ref[0, 0], prec_ref[...], 0.0)
    root = jnp.sqrt(weight)
    east = jnp.floor((column + 0.5) * (1.0 / cols_north))
    north = column - east * cols_north + (tile_north * cols_north).astype(F32) + 0.5
    east = east + (tile_east * cols_east).astype(F32) + 0.5
    numer = jnp.sum(weight * values * values, axis=1, keepdims=True)
    variance = jnp.sum(spread * spread, axis=0, keepdims=True)
    denom = jnp.sum(weight * variance, axis=1, keepdims=True) / (members - 1)
    out_ref[0:members, :] = spread * root
    row = lax.broadcasted_iota(jnp.int32, (ROWS - members, slots), 0)
    rest = jnp.zeros((ROWS - members, slots), F32)
    for place, value in enumerate((values * root, east, north, numer, denom)):
        rest = jnp.where(row == place, value, rest)
    out_ref[members:ROWS, :] = rest


def gram_kernel(members, cols_east, cols_north, obs_ref, out_ref, lhs_hi, lhs_lo, rhs_hi, rhs_lo):
    tiles = obs_ref.shape[0] // ROWS
    slots = obs_ref.shape[1]
    offsets, pull_row, total = pair_rows(members)
    regions_north = cols_north // SPAN
    deep = regions_north // 2 + 2
    lanes = 2 * LANES
    tile_east, tile_north = lax.axis_index("gx"), lax.axis_index("gy")
    count_north = lax.axis_size("gy")
    lane = lax.broadcasted_iota(jnp.int32, (1, lanes), 1)
    half = (lane >= LANES).astype(jnp.int32)
    inner = (lane - half * LANES).astype(F32)
    place_east = jnp.floor((inner + 0.5) / deep)
    place_north = inner - place_east * deep
    centre_east = (tile_east * cols_east).astype(F32) + (place_east - 1.0) * SPAN + 0.5 * SPAN
    place_north = place_north + (tile_north * regions_north + half * (regions_north // 2) - 1).astype(F32)
    place_north = jnp.clip(place_north, 0.0, float(count_north * regions_north - 1))
    centre_north = place_north * SPAN + 0.5 * SPAN
    period = float(lax.axis_size("gx") * cols_east)
    radius = float(cols_east)
    inv_radius = 1.0 / radius
    centre_north = centre_north * inv_radius

    def build(t):
        base = t * ROWS
        place = jnp.transpose(obs_ref[base + members : base + ROWS, :])
        east, north = place[:, 1:2], place[:, 2:3] * inv_radius
        away = jnp.abs(east - centre_east)
        away = jnp.minimum(away, period - away) * inv_radius
        up = north - centre_north
        near = jnp.maximum(1.0 - away * away - up * up, 0.0)
        taper = near * near
        span = slice(t * slots, (t + 1) * slots)
        hi = taper.astype(BF16)
        rhs_hi[span, :] = hi
        rhs_lo[span, :] = (taper - hi.astype(F32)).astype(BF16)
        for i in range(0, members, 2):
            first = (i // SUB) * SUB
            rows = obs_ref[base + first : base + members, :]
            table = jnp.concatenate(
                [obs_ref[base + i : base + i + 1, :] * rows, obs_ref[base + i + 1 : base + i + 2, :] * rows], axis=0
            )
            hi = table.astype(BF16)
            lhs_hi[offsets[i] : offsets[i] + table.shape[0], span] = hi
            lhs_lo[offsets[i] : offsets[i] + table.shape[0], span] = (table - hi.astype(F32)).astype(BF16)
        table = obs_ref[base + members : base + members + 1, :] * obs_ref[base : base + members, :]
        table = jnp.concatenate([table, jnp.zeros((total - pull_row - members, slots), F32)], axis=0)
        hi = table.astype(BF16)
        lhs_hi[pull_row:total, span] = hi
        lhs_lo[pull_row:total, span] = (table - hi.astype(F32)).astype(BF16)

    def multiply(t):
        span = slice(t * slots, (t + 1) * slots)
        left = jnp.concatenate([lhs_hi[:, span], lhs_lo[:, span], lhs_hi[:, span]], axis=1)
        right = jnp.concatenate([rhs_hi[span, :], rhs_hi[span, :], rhs_lo[span, :]], axis=0)
        return jnp.dot(left, right, preferred_element_type=F32)

    build(0)
    for t in range(tiles):
        if t + 1 < tiles:
            build(t + 1)
        if t == 0:
            out_ref[...] = multiply(t)
        else:
            out_ref[...] += multiply(t)


def gram_table(bundles, members, cols_east, cols_north):
    total = pair_rows(members)[2]
    deep = bundles.shape[0] // ROWS * bundles.shape[1]
    return pl.pallas_call(
        functools.partial(gram_kernel, members, cols_east, cols_north),
        out_shape=jax.ShapeDtypeStruct((total, 2 * LANES), F32),
        in_specs=[pl.BlockSpec(memory_space=pltpu.VMEM)],
        out_specs=pl.BlockSpec(memory_space=pltpu.VMEM),
        scratch_shapes=[
            pltpu.VMEM((total, deep), BF16),
            pltpu.VMEM((total, deep), BF16),
            pltpu.VMEM((deep, 2 * LANES), BF16),
            pltpu.VMEM((deep, 2 * LANES), BF16),
        ],
        compiler_params=pltpu.CompilerParams(vmem_limit_bytes=16 << 20),
        cost_estimate=pl.CostEstimate(flops=6 * total * deep * 2 * LANES, bytes_accessed=1 << 21, transcendentals=0),
        name="gram_table",
    )(bundles)


def columns_kernel(state_ref, out_ref, state_v, even_ref, odd_ref, in_sem):
    members, cols_east, cols_north, levels = state_v.shape
    pitch = even_ref.shape[0] // members

    def fetch(a):
        return pltpu.make_async_copy(state_ref.at[:, a], state_v.at[:, a], in_sem.at[a])

    for a in range(cols_east):
        fetch(a).start()
    gap = jnp.zeros((ROWS - members, levels), BF16)

    def load(a, ref):
        fetch(a).wait()
        for j in range(members):
            ref[j * pitch : j * pitch + cols_north, :] = state_v[j, a].astype(F32)

    def store(a, ref):
        for b in range(cols_north):
            column = ref[pl.ds(b, members, stride=pitch), :].astype(BF16)
            out_ref[a, b] = jnp.concatenate([column, gap], axis=0)

    def pair(t, carry):
        load(2 * t, even_ref)
        load(2 * t + 1, odd_ref)
        store(2 * t, even_ref)
        store(2 * t + 1, odd_ref)
        return carry

    lax.fori_loop(0, cols_east // 2, pair, 0)


def by_column(background):
    members, cols_east, cols_north, levels = background.shape
    shape = (cols_east, cols_north, ROWS, levels)
    return pl.pallas_call(
        columns_kernel,
        out_shape=jax.ShapeDtypeStruct(shape, BF16),
        in_specs=[pl.BlockSpec(memory_space=pltpu.HBM)],
        out_specs=pl.BlockSpec(memory_space=pltpu.VMEM),
        scratch_shapes=[
            pltpu.VMEM(background.shape, BF16),
            pltpu.VMEM((members * (cols_north + 1), levels), F32),
            pltpu.VMEM((members * (cols_north + 1), levels), F32),
            pltpu.SemaphoreType.DMA((cols_east,)),
        ],
        compiler_params=pltpu.CompilerParams(vmem_limit_bytes=20 << 20),
        cost_estimate=pl.CostEstimate(flops=0, bytes_accessed=12 << 20, transcendentals=0),
        name="columns",
    )(pltpu.with_memory_space_constraint(background, pltpu.HBM))


def analysis_kernel(
    members, grams, sums_a, sums_b, column_ref, out_ref, u_ref, v_ref, t_ref, s_ref, m_ref, w_ref, mean_ref, o_refs, out_v, out_sem
):
    _, cols_east, cols_north, levels = out_v.shape
    offsets, pull_row, _ = pair_rows(members)
    wide = 2 * LANES
    blocks = members // SUB
    pitch = cols_east * cols_north + 1
    half_cols = cols_north // 2
    half = cols_east * half_cols
    deep = half_cols // SPAN + 2

    def flush(a):
        return pltpu.make_async_copy(out_v.at[:, a], out_ref.at[:, a], out_sem.at[a])

    row = lax.broadcasted_iota(jnp.int32, (half, LANES), 0).astype(F32)
    lane = lax.broadcasted_iota(jnp.int32, (half, LANES), 1).astype(F32)
    col_east = jnp.floor((row + 0.5) / half_cols)
    col_north = row - col_east * half_cols
    reg_east = jnp.floor((lane + 0.5) / deep)
    reg_north = lane - reg_east * deep
    hat_east = jnp.maximum(1.0 - jnp.abs(col_east + 0.5 - ((reg_east - 1.0) * SPAN + 0.5 * SPAN)) / SPAN, 0.0)
    hat_north = jnp.maximum(1.0 - jnp.abs(col_north + 0.5 - ((reg_north - 1.0) * SPAN + 0.5 * SPAN)) / SPAN, 0.0)
    hats = (hat_east * hat_north).astype(BF16)
    w_ref[:, 0:LANES] = hats
    w_ref[:, LANES:wide] = hats

    total = sums_a[...] + sums_b[...]
    prior = (members - 1) / (total[0:1, 0:1] / total[1:2, 0:1])
    sub = lax.broadcasted_iota(jnp.int32, (SUB, wide), 0)
    gap = jnp.zeros((SLOT - ROWS, wide), BF16)
    fold = -(-members // (2 * SUB)) * SUB

    def gram(row0):
        return functools.reduce(lambda x, y: x + y, [g[row0 : row0 + SUB, :] for g in grams])

    def part(h, k):
        return t_ref[h, k * ROWS : (k + 1) * ROWS, :]

    def put(k, blocks_k):
        table = jnp.concatenate(blocks_k + [jnp.zeros((ROWS - members, wide), F32)], axis=0)
        hi = table.astype(BF16)
        lo = (table - hi.astype(F32)).astype(BF16)
        for h in range(2):
            t_ref[h, k * ROWS : (k + 1) * ROWS, 0:LANES] = hi[:, h * LANES : (h + 1) * LANES]
            t_ref[h, k * ROWS : (k + 1) * ROWS, LANES:wide] = lo[:, h * LANES : (h + 1) * LANES]

    def spread(h, right):
        return lax.dot_general(w_ref[...], right, (((1,), (1,)), ((), ())), preferred_element_type=F32)

    scale = math.sqrt(members - 1)
    mean_ref[...] = jnp.zeros_like(mean_ref)

    def factor_rows(start, stop):
        for i in range(start, stop):
            own = i // SUB
            acc_u = [gram(offsets[i] + SUB * b) for b in range(blocks - own)]
            at = sub == i % SUB
            acc_u[0] = acc_u[0] + jnp.where(at, prior, 0.0)
            acc_v = [jnp.zeros((SUB, wide), F32) for _ in range(own)] + [jnp.where(at, 1.0, 0.0)]
            for p in range(i):
                row = p * members
                factor = u_ref[row + i : row + i + 1, :]
                for b in range(own, blocks):
                    acc_u[b - own] = acc_u[b - own] - factor * u_ref[row + SUB * b : row + SUB * (b + 1), :]
                for b in range(p // SUB + 1):
                    acc_v[b] = acc_v[b] - factor * v_ref[row + SUB * b : row + SUB * (b + 1), :]
            inv = lax.rsqrt(acc_u[0][i % SUB : i % SUB + 1, :])
            for b in range(own, blocks):
                u_ref[i * members + SUB * b : i * members + SUB * (b + 1), :] = acc_u[b - own] * inv
            for b in range(own + 1):
                v_ref[i * members + SUB * b : i * members + SUB * (b + 1), :] = acc_v[b] * inv

    def put_rows(start, stop):
        most = (stop - 1) // SUB + 1
        pulls = [gram(pull_row + SUB * b) for b in range(most)]
        mean_w = [mean_ref[SUB * b : SUB * (b + 1), :] for b in range(most)]
        for i in range(start, stop):
            count = i // SUB + 1
            rows = [v_ref[i * members + SUB * b : i * members + SUB * (b + 1), :] for b in range(count)]
            solved = functools.reduce(lambda x, y: x + y, [x * y for x, y in zip(rows, pulls)])
            solved = jnp.sum(solved, axis=0, keepdims=True)
            shift = jnp.sum(functools.reduce(lambda x, y: x + y, rows), axis=0, keepdims=True) * (-scale / members)
            for b in range(count):
                mean_w[b] = mean_w[b] + solved * rows[b]
            rows = [x * scale + shift for x in rows]
            put(i, rows + [jnp.broadcast_to(shift, (SUB, wide))] * (blocks - count))
        for b in range(most):
            mean_ref[SUB * b : SUB * (b + 1), :] = mean_w[b]

    def spread_rows(k):
        for h in range(2):
            sides = []
            for n in (k, k + 1):
                other = part(h, n + fold) if n + fold < members else jnp.zeros((ROWS, wide), BF16)
                sides += [part(h, n), gap, other, gap]
            both = spread(h, jnp.concatenate(sides, axis=0))
            s_ref[k * pitch + h * half : k * pitch + (h + 1) * half, :] = both[:, 0:LANES]
            s_ref[(k + 1) * pitch + h * half : (k + 1) * pitch + (h + 1) * half, :] = both[:, LANES:wide]

    def spread_mean():
        mean_w = [mean_ref[SUB * b : SUB * (b + 1), :] for b in range(blocks)]
        mean_sum = jnp.sum(functools.reduce(lambda x, y: x + y, mean_w), axis=0, keepdims=True)
        shift = (1.0 - mean_sum) * (1.0 / members)
        put(members, [x + shift for x in mean_w])
        for h in range(2):
            right = jnp.concatenate([part(h, members), gap, part(h, members), gap], axis=0)
            m_ref[h * half : (h + 1) * half, :] = spread(h, right)

    for i in range(members):
        factor_rows(i, i + 1)
        put_rows(i, i + 1)
        if i % 2 and i >= fold:
            spread_rows(i - fold - 1)
    for k in range(members - fold, fold, 2):
        spread_rows(k)
    spread_mean()
    lower_lane = lax.broadcasted_iota(jnp.int32, (fold, LANES), 1) < SLOT
    blank = jnp.zeros((SLOT - ROWS, 2 * levels), BF16)
    pitch_o = members + 1

    def matrix(a, b):
        h, within = b // half_cols, b % half_cols
        place = h * half + a * half_cols + within
        value = s_ref[pl.ds(place, fold, stride=pitch), :] + m_ref[pl.ds(place, 1), :]
        high = value.astype(BF16).astype(F32)
        low = value - high
        turned = pltpu.roll(jnp.where(lower_lane, low, high), SLOT, 1)
        first = jnp.where(lower_lane, high, turned)
        second = jnp.where(lower_lane, turned, low)
        return [first, second[0 : members - fold, :]]

    def apply(a, b, o_ref):
        left = jnp.concatenate(matrix(a, b) + matrix(a, b + 1), axis=0).astype(BF16)
        right = jnp.concatenate([column_ref[a, b], column_ref[a, b + 1]], axis=1)
        right = jnp.concatenate([right, blank, right, blank], axis=0)
        both = jnp.dot(left, right, preferred_element_type=F32)
        o_ref[b * pitch_o : b * pitch_o + members, :] = both[:members, 0:levels]
        o_ref[(b + 1) * pitch_o : (b + 1) * pitch_o + members, :] = both[members:, levels:]

    def emit(a, k, o_ref):
        out_v[k, a] = o_ref[pl.ds(k, cols_north, stride=pitch_o), :].astype(BF16)

    def step(a, to_ref, from_ref):
        done = 0
        for b in range(0, cols_north, 2):
            if to_ref is not None:
                apply(a, b, to_ref)
            if from_ref is not None:
                upto = members * (b + 2) // cols_north
                for k in range(done, upto):
                    emit(a - 1, k, from_ref)
                done = upto
        if from_ref is not None:
            flush(a - 1).start()

    even, odd = o_refs
    step(0, even, None)

    def column_rows(t, carry):
        step(2 * t + 1, odd, even)
        step(2 * t + 2, even, odd)
        return carry

    lax.fori_loop(0, cols_east // 2 - 1, column_rows, 0)
    step(cols_east - 1, odd, even)
    step(cols_east, None, odd)
    for a in range(cols_east):
        flush(a).wait()


def analyse(grams, sums_a, sums_b, columns, members):
    cols_east, cols_north, _, levels = columns.shape
    count = cols_east * cols_north
    tables = len(grams)

    def body(*refs):
        rest = refs[tables:]
        analysis_kernel(members, refs[:tables], *rest[:11], rest[11:13], *rest[13:])

    vmem = pl.BlockSpec(memory_space=pltpu.VMEM)
    hbm = pl.BlockSpec(memory_space=pltpu.HBM)
    pitch = count + 1
    shape = (members, cols_east, cols_north, levels)
    return pl.pallas_call(
        body,
        out_shape=jax.ShapeDtypeStruct(shape, BF16),
        in_specs=[vmem] * (tables + 3),
        out_specs=hbm,
        scratch_shapes=[
            pltpu.VMEM((members * members, 2 * LANES), F32),
            pltpu.VMEM((members * members, 2 * LANES), F32),
            pltpu.VMEM((2, (members + 1) * ROWS, 2 * LANES), BF16),
            pltpu.VMEM((-(-members // (2 * SUB)) * SUB * pitch, LANES), F32),
            pltpu.VMEM((count, LANES), F32),
            pltpu.VMEM((count // 2, 2 * LANES), BF16),
            pltpu.VMEM((members, 2 * LANES), F32),
            pltpu.VMEM((cols_north * (members + 1), levels), F32),
            pltpu.VMEM((cols_north * (members + 1), levels), F32),
            pltpu.VMEM(shape, BF16),
            pltpu.SemaphoreType.DMA((cols_east,)),
        ],
        compiler_params=pltpu.CompilerParams(vmem_limit_bytes=30 << 20),
        name="analyse",
    )(*grams, sums_a, sums_b, columns)


def rotate(value, axis, step):
    count = lax.axis_size(axis)
    return lax.ppermute(value, axis, [(i, (i + step) % count) for i in range(count)])


def slide(value, axis, step):
    count = lax.axis_size(axis)
    return lax.ppermute(value, axis, [(i, i + step) for i in range(count) if 0 <= i + step < count])


def swap(value, axis, bit):
    count = lax.axis_size(axis)
    return lax.ppermute(value, axis, [(i, i ^ bit) for i in range(count)])


def per_device(background, obs_perturb, innovation, obs_precision, obs_column, obs_count):
    members, cols_east, cols_north, levels = background.shape
    slots = obs_perturb.shape[3]
    count_east, count_north = lax.axis_size("gx"), lax.axis_size("gy")
    vmem = pl.BlockSpec(memory_space=pltpu.VMEM)
    hbm = pl.BlockSpec(memory_space=pltpu.HBM)
    inputs = (obs_perturb[0, 0], innovation[0], obs_precision[0], obs_column[0])
    bundle = pl.pallas_call(
        functools.partial(prep_kernel, cols_east, cols_north),
        out_shape=jax.ShapeDtypeStruct((ROWS, slots), F32),
        in_specs=[pl.BlockSpec(memory_space=pltpu.SMEM)] + [hbm] * 4,
        out_specs=vmem,
        scratch_shapes=[pltpu.VMEM(x.shape, x.dtype) for x in inputs] + [pltpu.SemaphoreType.DMA((4,))],
        compiler_params=pltpu.CompilerParams(vmem_limit_bytes=2 << 20),
        name="prep",
    )(obs_count, *(pltpu.with_memory_space_constraint(x, pltpu.HBM) for x in inputs))
    steps = sorted({s % count_east for s in (-2, -1, 1, 2)} - {0})
    around = [rotate(bundle, "gx", s) for s in steps]
    columns = by_column(background)
    own = jnp.concatenate([bundle] + around, axis=0)
    below = slide(own, "gy", 1)
    above = slide(own, "gy", -1)

    def row_sum(bundles):
        each = bundles.reshape(-1, ROWS, slots)[:, members + 3 : members + 5, 0:LANES]
        return jnp.sum(each, axis=0)

    if len(steps) + 1 == count_east and count_north == 8:
        mine = row_sum(own)
        far = swap(mine, "gy", 2), swap(mine, "gy", 4)
        beside = jnp.where(lax.axis_index("gy") % 2 == 0, row_sum(above), row_sum(below))
        total = (mine + beside) + (far[0] + far[1])
        other = swap(total, "gy", 7)
    else:
        total = lax.psum(bundle[members + 3 : members + 5, 0:LANES], ("gx", "gy"))
        other = jnp.zeros_like(total)
    grams = [gram_table(x, members, cols_east, cols_north) for x in (own, below, above)]
    return analyse(grams, total, other, columns, members)


def solution(mesh):
    return jax.shard_map(
        per_device,
        mesh=mesh,
        in_specs=(
            P(None, "gx", "gy", None),
            P("gx", "gy", None, None),
            P("gx", "gy", None),
            P("gx", "gy", None),
            P("gx", "gy", None),
            P("gx", "gy"),
        ),
        out_specs=P(None, "gx", "gy", None),
        check_vma=False,
    )
```

```python
import functools
import math

import jax
import jax.numpy as jnp
from jax import lax
from jax.experimental import pallas as pl
from jax.experimental.pallas import tpu as pltpu
from jax.sharding import PartitionSpec as P

SPAN = 2
LANES = 128
SUB = 8
ROWS = 48
SLOT = 64
F32 = jnp.float32
BF16 = jnp.bfloat16


def pair_rows(members):
    offsets, total = [], 0
    for i in range(members):
        offsets.append(total)
        total += members - (i // SUB) * SUB
    pull = total
    total += members
    return offsets, pull, -(-total // 16) * 16


def prep_kernel(
    cols_east, cols_north, count_ref, perturb_hbm, innov_hbm, prec_hbm, column_hbm, out_ref,
    perturb_ref, innov_ref, prec_ref, column_ref, sem,
):
    pairs = ((perturb_hbm, perturb_ref), (innov_hbm, innov_ref), (prec_hbm, prec_ref), (column_hbm, column_ref))
    copies = [pltpu.make_async_copy(src, dst, sem.at[n]) for n, (src, dst) in enumerate(pairs)]
    for copy in copies:
        copy.start()
    for copy in copies:
        copy.wait()
    members, slots = perturb_ref.shape
    tile_east, tile_north = lax.axis_index("gx"), lax.axis_index("gy")
    values, column = innov_ref[...], column_ref[...].astype(F32)
    spread = perturb_ref[...].astype(F32)
    spread = spread - jnp.sum(spread, axis=0, keepdims=True) / members
    lane = lax.broadcasted_iota(jnp.int32, (1, slots), 1)
    weight = jnp.where(lane < count_ref[0, 0], prec_ref[...], 0.0)
    root = jnp.sqrt(weight)
    east = jnp.floor((column + 0.5) * (1.0 / cols_north))
    north = column - east * cols_north + (tile_north * cols_north).astype(F32) + 0.5
    east = east + (tile_east * cols_east).astype(F32) + 0.5
    numer = jnp.sum(weight * values * values, axis=1, keepdims=True)
    variance = jnp.sum(spread * spread, axis=0, keepdims=True)
    denom = jnp.sum(weight * variance, axis=1, keepdims=True) / (members - 1)
    out_ref[0:members, :] = spread * root
    row = lax.broadcasted_iota(jnp.int32, (ROWS - members, slots), 0)
    rest = jnp.zeros((ROWS - members, slots), F32)
    for place, value in enumerate((values * root, east, north, numer, denom)):
        rest = jnp.where(row == place, value, rest)
    out_ref[members:ROWS, :] = rest


def gram_kernel(members, cols_east, cols_north, obs_ref, out_ref, lhs_hi, lhs_lo, rhs_hi, rhs_lo):
    tiles = obs_ref.shape[0] // ROWS
    slots = obs_ref.shape[1]
    offsets, pull_row, total = pair_rows(members)
    regions_north = cols_north // SPAN
    deep = regions_north // 2 + 2
    lanes = 2 * LANES
    tile_east, tile_north = lax.axis_index("gx"), lax.axis_index("gy")
    count_north = lax.axis_size("gy")
    lane = lax.broadcasted_iota(jnp.int32, (1, lanes), 1)
    half = (lane >= LANES).astype(jnp.int32)
    inner = (lane - half * LANES).astype(F32)
    place_east = jnp.floor((inner + 0.5) / deep)
    place_north = inner - place_east * deep
    centre_east = (tile_east * cols_east).astype(F32) + (place_east - 1.0) * SPAN + 0.5 * SPAN
    place_north = place_north + (tile_north * regions_north + half * (regions_north // 2) - 1).astype(F32)
    place_north = jnp.clip(place_north, 0.0, float(count_north * regions_north - 1))
    centre_north = place_north * SPAN + 0.5 * SPAN
    period = float(lax.axis_size("gx") * cols_east)
    radius = float(cols_east)
    inv_radius = 1.0 / radius
    centre_north = centre_north * inv_radius

    def build(t):
        base = t * ROWS
        place = jnp.transpose(obs_ref[base + members : base + ROWS, :])
        east, north = place[:, 1:2], place[:, 2:3] * inv_radius
        away = jnp.abs(east - centre_east)
        away = jnp.minimum(away, period - away) * inv_radius
        up = north - centre_north
        near = jnp.maximum(1.0 - away * away - up * up, 0.0)
        taper = near * near
        span = slice(t * slots, (t + 1) * slots)
        hi = taper.astype(BF16)
        rhs_hi[span, :] = hi
        rhs_lo[span, :] = (taper - hi.astype(F32)).astype(BF16)
        for i in range(0, members, 2):
            first = (i // SUB) * SUB
            rows = obs_ref[base + first : base + members, :]
            table = jnp.concatenate(
                [obs_ref[base + i : base + i + 1, :] * rows, obs_ref[base + i + 1 : base + i + 2, :] * rows], axis=0
            )
            hi = table.astype(BF16)
            lhs_hi[offsets[i] : offsets[i] + table.shape[0], span] = hi
            lhs_lo[offsets[i] : offsets[i] + table.shape[0], span] = (table - hi.astype(F32)).astype(BF16)
        table = obs_ref[base + members : base + members + 1, :] * obs_ref[base : base + members, :]
        table = jnp.concatenate([table, jnp.zeros((total - pull_row - members, slots), F32)], axis=0)
        hi = table.astype(BF16)
        lhs_hi[pull_row:total, span] = hi
        lhs_lo[pull_row:total, span] = (table - hi.astype(F32)).astype(BF16)

    def multiply(t):
        span = slice(t * slots, (t + 1) * slots)
        left = jnp.concatenate([lhs_hi[:, span], lhs_lo[:, span], lhs_hi[:, span]], axis=1)
        right = jnp.concatenate([rhs_hi[span, :], rhs_hi[span, :], rhs_lo[span, :]], axis=0)
        return jnp.dot(left, right, preferred_element_type=F32)

    build(0)
    for t in range(tiles):
        if t + 1 < tiles:
            build(t + 1)
        if t == 0:
            out_ref[...] = multiply(t)
        else:
            out_ref[...] += multiply(t)


def gram_table(bundles, members, cols_east, cols_north):
    total = pair_rows(members)[2]
    deep = bundles.shape[0] // ROWS * bundles.shape[1]
    return pl.pallas_call(
        functools.partial(gram_kernel, members, cols_east, cols_north),
        out_shape=jax.ShapeDtypeStruct((total, 2 * LANES), F32),
        in_specs=[pl.BlockSpec(memory_space=pltpu.VMEM)],
        out_specs=pl.BlockSpec(memory_space=pltpu.VMEM),
        scratch_shapes=[
            pltpu.VMEM((total, deep), BF16),
            pltpu.VMEM((total, deep), BF16),
            pltpu.VMEM((deep, 2 * LANES), BF16),
            pltpu.VMEM((deep, 2 * LANES), BF16),
        ],
        compiler_params=pltpu.CompilerParams(vmem_limit_bytes=16 << 20),
        cost_estimate=pl.CostEstimate(flops=6 * total * deep * 2 * LANES, bytes_accessed=1 << 21, transcendentals=0),
        name="gram_table",
    )(bundles)


def columns_kernel(state_ref, out_ref, state_v, even_ref, odd_ref, in_sem):
    members, cols_east, cols_north, levels = state_v.shape
    pitch = even_ref.shape[0] // members

    def fetch(a):
        return pltpu.make_async_copy(state_ref.at[:, a], state_v.at[:, a], in_sem.at[a])

    for a in range(cols_east):
        fetch(a).start()
    gap = jnp.zeros((ROWS - members, levels), BF16)

    def load(a, ref):
        fetch(a).wait()
        for j in range(members):
            ref[j * pitch : j * pitch + cols_north, :] = state_v[j, a].astype(F32)

    def store(a, ref):
        for b in range(cols_north):
            column = ref[pl.ds(b, members, stride=pitch), :].astype(BF16)
            out_ref[a, b] = jnp.concatenate([column, gap], axis=0)

    def pair(t, carry):
        load(2 * t, even_ref)
        load(2 * t + 1, odd_ref)
        store(2 * t, even_ref)
        store(2 * t + 1, odd_ref)
        return carry

    lax.fori_loop(0, cols_east // 2, pair, 0)


def by_column(background):
    members, cols_east, cols_north, levels = background.shape
    shape = (cols_east, cols_north, ROWS, levels)
    return pl.pallas_call(
        columns_kernel,
        out_shape=jax.ShapeDtypeStruct(shape, BF16),
        in_specs=[pl.BlockSpec(memory_space=pltpu.HBM)],
        out_specs=pl.BlockSpec(memory_space=pltpu.VMEM),
        scratch_shapes=[
            pltpu.VMEM(background.shape, BF16),
            pltpu.VMEM((members * (cols_north + 1), levels), F32),
            pltpu.VMEM((members * (cols_north + 1), levels), F32),
            pltpu.SemaphoreType.DMA((cols_east,)),
        ],
        compiler_params=pltpu.CompilerParams(vmem_limit_bytes=20 << 20),
        cost_estimate=pl.CostEstimate(flops=0, bytes_accessed=12 << 20, transcendentals=0),
        name="columns",
    )(pltpu.with_memory_space_constraint(background, pltpu.HBM))


def analysis_kernel(
    members, grams, sums_a, sums_b, column_ref, out_ref, u_ref, v_ref, t_ref, s_ref, m_ref, w_ref, mean_ref, l_ref, o_refs, out_v, out_sem
):
    _, cols_east, cols_north, levels = out_v.shape
    offsets, pull_row, _ = pair_rows(members)
    wide = 2 * LANES
    blocks = members // SUB
    pitch = cols_east * cols_north + 1
    half_cols = cols_north // 2
    half = cols_east * half_cols
    deep = half_cols // SPAN + 2

    def flush(a):
        return pltpu.make_async_copy(out_v.at[:, a], out_ref.at[:, a], out_sem.at[a])

    row = lax.broadcasted_iota(jnp.int32, (half, LANES), 0).astype(F32)
    lane = lax.broadcasted_iota(jnp.int32, (half, LANES), 1).astype(F32)
    col_east = jnp.floor((row + 0.5) / half_cols)
    col_north = row - col_east * half_cols
    reg_east = jnp.floor((lane + 0.5) / deep)
    reg_north = lane - reg_east * deep
    hat_east = jnp.maximum(1.0 - jnp.abs(col_east + 0.5 - ((reg_east - 1.0) * SPAN + 0.5 * SPAN)) / SPAN, 0.0)
    hat_north = jnp.maximum(1.0 - jnp.abs(col_north + 0.5 - ((reg_north - 1.0) * SPAN + 0.5 * SPAN)) / SPAN, 0.0)
    hats = (hat_east * hat_north).astype(BF16)
    w_ref[:, 0:LANES] = hats
    w_ref[:, LANES:wide] = hats

    total = sums_a[...] + sums_b[...]
    prior = (members - 1) / (total[0:1, 0:1] / total[1:2, 0:1])
    sub = lax.broadcasted_iota(jnp.int32, (SUB, wide), 0)
    gap = jnp.zeros((SLOT - ROWS, wide), BF16)
    fold = -(-members // (2 * SUB)) * SUB

    def gram(row0):
        return functools.reduce(lambda x, y: x + y, [g[row0 : row0 + SUB, :] for g in grams])

    def part(h, k):
        return t_ref[h, k * ROWS : (k + 1) * ROWS, :]

    def put(k, blocks_k):
        table = jnp.concatenate(blocks_k + [jnp.zeros((ROWS - members, wide), F32)], axis=0)
        hi = table.astype(BF16)
        lo = (table - hi.astype(F32)).astype(BF16)
        for h in range(2):
            t_ref[h, k * ROWS : (k + 1) * ROWS, 0:LANES] = hi[:, h * LANES : (h + 1) * LANES]
            t_ref[h, k * ROWS : (k + 1) * ROWS, LANES:wide] = lo[:, h * LANES : (h + 1) * LANES]

    def spread(h, right):
        return lax.dot_general(w_ref[...], right, (((1,), (1,)), ((), ())), preferred_element_type=F32)

    scale = math.sqrt(members - 1)
    mean_ref[...] = jnp.zeros_like(mean_ref)

    def factor_rows(start, stop):
        for i in range(start, stop):
            own = i // SUB
            acc_u = [gram(offsets[i] + SUB * b) for b in range(blocks - own)]
            at = sub == i % SUB
            acc_u[0] = acc_u[0] + jnp.where(at, prior, 0.0)
            acc_v = [jnp.zeros((SUB, wide), F32) for _ in range(own)] + [jnp.where(at, scale, 0.0)]
            for p in range(i):
                row = p * members
                factor = u_ref[row + i : row + i + 1, :]
                for b in range(own, blocks):
                    acc_u[b - own] = acc_u[b - own] - factor * u_ref[row + SUB * b : row + SUB * (b + 1), :]
                for b in range(p // SUB + 1):
                    acc_v[b] = acc_v[b] - factor * v_ref[row + SUB * b : row + SUB * (b + 1), :]
            inv = lax.rsqrt(acc_u[0][i % SUB : i % SUB + 1, :])
            for b in range(own, blocks):
                u_ref[i * members + SUB * b : i * members + SUB * (b + 1), :] = acc_u[b - own] * inv
            for b in range(own + 1):
                v_ref[i * members + SUB * b : i * members + SUB * (b + 1), :] = acc_v[b] * inv

    def put_rows(start, stop):
        most = (stop - 1) // SUB + 1
        pulls = [gram(pull_row + SUB * b) * (1.0 / (members - 1)) for b in range(most)]
        mean_w = [mean_ref[SUB * b : SUB * (b + 1), :] for b in range(most)]
        for i in range(start, stop):
            count = i // SUB + 1
            rows = [v_ref[i * members + SUB * b : i * members + SUB * (b + 1), :] for b in range(count)]
            solved = functools.reduce(lambda x, y: x + y, [x * y for x, y in zip(rows, pulls)])
            solved = jnp.sum(solved, axis=0, keepdims=True)
            shift = jnp.sum(functools.reduce(lambda x, y: x + y, rows), axis=0, keepdims=True) * (-1.0 / members)
            for b in range(count):
                mean_w[b] = mean_w[b] + solved * rows[b]
            rows = [x + shift for x in rows]
            put(i, rows + [jnp.broadcast_to(shift, (SUB, wide))] * (blocks - count))
        for b in range(most):
            mean_ref[SUB * b : SUB * (b + 1), :] = mean_w[b]

    def spread_rows(k):
        for h in range(2):
            sides = []
            for n in (k, k + 1):
                other = part(h, n + fold) if n + fold < members else jnp.zeros((ROWS, wide), BF16)
                sides += [part(h, n), gap, other, gap]
            both = spread(h, jnp.concatenate(sides, axis=0))
            s_ref[k * pitch + h * half : k * pitch + (h + 1) * half, :] = both[:, 0:LANES]
            s_ref[(k + 1) * pitch + h * half : (k + 1) * pitch + (h + 1) * half, :] = both[:, LANES:wide]

    def spread_mean():
        mean_w = [mean_ref[SUB * b : SUB * (b + 1), :] for b in range(blocks)]
        mean_sum = jnp.sum(functools.reduce(lambda x, y: x + y, mean_w), axis=0, keepdims=True)
        shift = (1.0 - mean_sum) * (1.0 / members)
        put(members, [x + shift for x in mean_w])
        for h in range(2):
            right = jnp.concatenate([part(h, members), gap, part(h, members), gap], axis=0)
            m_ref[h * half : (h + 1) * half, :] = spread(h, right)

    for i in range(members):
        factor_rows(i, i + 1)
        put_rows(i, i + 1)
        if i % 2 and i >= fold:
            spread_rows(i - fold - 1)
    for k in range(members - fold, fold, 2):
        spread_rows(k)
    spread_mean()
    lower_lane = lax.broadcasted_iota(jnp.int32, (fold, LANES), 1) < SLOT
    blank = jnp.zeros((SLOT - ROWS, 2 * levels), BF16)
    pitch_o = members + 1

    def matrix(a, b):
        h, within = b // half_cols, b % half_cols
        place = h * half + a * half_cols + within
        value = s_ref[pl.ds(place, fold, stride=pitch), :] + m_ref[pl.ds(place, 1), :]
        high = value.astype(BF16).astype(F32)
        low = value - high
        turned = pltpu.roll(jnp.where(lower_lane, low, high), SLOT, 1)
        first = jnp.where(lower_lane, high, turned)
        second = jnp.where(lower_lane, turned, low)
        return [first, second[0 : members - fold, :]]

    def prepare(a, b, slot):
        left = jnp.concatenate(matrix(a, b) + matrix(a, b + 1), axis=0).astype(BF16)
        l_ref[slot, b // 2] = left

    def apply(a, b, slot, o_ref):
        right = jnp.concatenate([column_ref[a, b], column_ref[a, b + 1]], axis=1)
        right = jnp.concatenate([right, blank, right, blank], axis=0)
        both = jnp.dot(l_ref[slot, b // 2], right, preferred_element_type=F32)
        o_ref[b * pitch_o : b * pitch_o + members, :] = both[:members, 0:levels]
        o_ref[(b + 1) * pitch_o : (b + 1) * pitch_o + members, :] = both[members:, levels:]

    def emit(a, k, o_ref):
        out_v[k, a] = o_ref[pl.ds(k, cols_north, stride=pitch_o), :].astype(BF16)

    group = 4

    def column_rows(t, carry):
        for s in range(group):
            a = group * t + s
            done = 0
            for b in range(0, cols_north, 2):
                apply(a, b, s % 2, o_refs[s % 2])
                prepare(jnp.minimum(a + 1, cols_east - 1), b, (s + 1) % 2)
                upto = members * (b + 2) // cols_north
                if s:
                    for k in range(done, upto):
                        emit(a - 1, k, o_refs[(s - 1) % 2])
                done = upto
            if s:
                flush(a - 1).start()
        a = group * t + group - 1
        for k in range(members):
            emit(a, k, o_refs[(group - 1) % 2])
        flush(a).start()
        return carry

    for b in range(0, cols_north, 2):
        prepare(0, b, 0)
    lax.fori_loop(0, cols_east // group, column_rows, 0)
    for a in range(cols_east):
        flush(a).wait()


def analyse(grams, sums_a, sums_b, columns, members):
    cols_east, cols_north, _, levels = columns.shape
    count = cols_east * cols_north
    tables = len(grams)

    def body(*refs):
        rest = refs[tables:]
        analysis_kernel(members, refs[:tables], *rest[:12], rest[12:14], *rest[14:])

    vmem = pl.BlockSpec(memory_space=pltpu.VMEM)
    hbm = pl.BlockSpec(memory_space=pltpu.HBM)
    pitch = count + 1
    shape = (members, cols_east, cols_north, levels)
    return pl.pallas_call(
        body,
        out_shape=jax.ShapeDtypeStruct(shape, BF16),
        in_specs=[vmem] * (tables + 3),
        out_specs=hbm,
        scratch_shapes=[
            pltpu.VMEM((members * members, 2 * LANES), F32),
            pltpu.VMEM((members * members, 2 * LANES), F32),
            pltpu.VMEM((2, (members + 1) * ROWS, 2 * LANES), BF16),
            pltpu.VMEM((-(-members // (2 * SUB)) * SUB * pitch, LANES), F32),
            pltpu.VMEM((count, LANES), F32),
            pltpu.VMEM((count // 2, 2 * LANES), BF16),
            pltpu.VMEM((members, 2 * LANES), F32),
            pltpu.VMEM((2, cols_north // 2, 2 * members, LANES), BF16),
            pltpu.VMEM((cols_north * (members + 1), levels), F32),
            pltpu.VMEM((cols_north * (members + 1), levels), F32),
            pltpu.VMEM(shape, BF16),
            pltpu.SemaphoreType.DMA((cols_east,)),
        ],
        compiler_params=pltpu.CompilerParams(vmem_limit_bytes=30 << 20),
        name="analyse",
    )(*grams, sums_a, sums_b, columns)


def rotate(value, axis, step):
    count = lax.axis_size(axis)
    return lax.ppermute(value, axis, [(i, (i + step) % count) for i in range(count)])


def swap(value, axis, bits):
    count = lax.axis_size(axis)
    return lax.ppermute(value, axis, [(i, i ^ bits) for i in range(count) if i ^ bits < count])


def swap_beside(value, axis):
    count = lax.axis_size(axis)
    pairs = [(i, ((i + 1) ^ 1) - 1) for i in range(count)]
    return lax.ppermute(value, axis, [(i, j) for i, j in pairs if 0 <= j < count])


def per_device(background, obs_perturb, innovation, obs_precision, obs_column, obs_count):
    members, cols_east, cols_north, levels = background.shape
    slots = obs_perturb.shape[3]
    count_east, count_north = lax.axis_size("gx"), lax.axis_size("gy")
    vmem = pl.BlockSpec(memory_space=pltpu.VMEM)
    hbm = pl.BlockSpec(memory_space=pltpu.HBM)
    inputs = (obs_perturb[0, 0], innovation[0], obs_precision[0], obs_column[0])
    bundle = pl.pallas_call(
        functools.partial(prep_kernel, cols_east, cols_north),
        out_shape=jax.ShapeDtypeStruct((ROWS, slots), F32),
        in_specs=[pl.BlockSpec(memory_space=pltpu.SMEM)] + [hbm] * 4,
        out_specs=vmem,
        scratch_shapes=[pltpu.VMEM(x.shape, x.dtype) for x in inputs] + [pltpu.SemaphoreType.DMA((4,))],
        compiler_params=pltpu.CompilerParams(vmem_limit_bytes=2 << 20),
        name="prep",
    )(obs_count, *(pltpu.with_memory_space_constraint(x, pltpu.HBM) for x in inputs))
    steps = sorted({s % count_east for s in (-2, -1, 1, 2)} - {0})
    if count_east == 4:
        around = [swap(bundle, "gx", bits) for bits in (3, 2, 1)]
    else:
        around = [rotate(bundle, "gx", s) for s in steps]
    *around, columns = lax.optimization_barrier((*around, by_column(background)))
    own = jnp.concatenate([bundle] + around, axis=0)
    beside = swap_beside(own, "gy")
    partner = swap(own, "gy", 1)

    def row_sum(bundles):
        each = bundles.reshape(-1, ROWS, slots)[:, members + 3 : members + 5, 0:LANES]
        return jnp.sum(each, axis=0)

    table = functools.partial(gram_table, members=members, cols_east=cols_east, cols_north=cols_north)
    if len(steps) + 1 == count_east and count_north == 8:
        total = row_sum(own) + row_sum(partner)
        own, total = lax.optimization_barrier((own, total))
        total = total + swap(total, "gy", 2)
        first = table(own)
        partner, total = lax.optimization_barrier((partner, total))
        other = swap(total, "gy", 4)
        grams = [first, table(partner), table(beside)]
    else:
        total = lax.psum(bundle[members + 3 : members + 5, 0:LANES], ("gx", "gy"))
        other = jnp.zeros_like(total)
        grams = [table(x) for x in (own, partner, beside)]
    return analyse(grams, total, other, columns, members)


def solution(mesh):
    return jax.shard_map(
        per_device,
        mesh=mesh,
        in_specs=(
            P(None, "gx", "gy", None),
            P("gx", "gy", None, None),
            P("gx", "gy", None),
            P("gx", "gy", None),
            P("gx", "gy", None),
            P("gx", "gy"),
        ),
        out_specs=P(None, "gx", "gy", None),
        check_vma=False,
    )
```

```python
import functools
import math

import jax
import jax.numpy as jnp
from jax import lax
from jax.experimental import pallas as pl
from jax.experimental.pallas import tpu as pltpu
from jax.sharding import PartitionSpec as P

SPAN = 2
LANES = 128
SUB = 8
ROWS = 48
SLOT = 64
F32 = jnp.float32
BF16 = jnp.bfloat16


def pair_rows(members):
    offsets, total = [], 0
    for i in range(members):
        offsets.append(total)
        total += members - (i // SUB) * SUB
    pull = total
    total += members
    return offsets, pull, -(-total // 16) * 16


def prep_kernel(
    cols_east, cols_north, count_ref, perturb_hbm, innov_hbm, prec_hbm, column_hbm, out_ref,
    perturb_ref, innov_ref, prec_ref, column_ref, sem,
):
    pairs = ((perturb_hbm, perturb_ref), (innov_hbm, innov_ref), (prec_hbm, prec_ref), (column_hbm, column_ref))
    copies = [pltpu.make_async_copy(src, dst, sem.at[n]) for n, (src, dst) in enumerate(pairs)]
    for copy in copies:
        copy.start()
    for copy in copies:
        copy.wait()
    members, slots = perturb_ref.shape
    tile_east, tile_north = lax.axis_index("gx"), lax.axis_index("gy")
    values, column = innov_ref[...], column_ref[...].astype(F32)
    spread = perturb_ref[...].astype(F32)
    spread = spread - jnp.sum(spread, axis=0, keepdims=True) / members
    lane = lax.broadcasted_iota(jnp.int32, (1, slots), 1)
    weight = jnp.where(lane < count_ref[0, 0], prec_ref[...], 0.0)
    root = jnp.sqrt(weight)
    east = jnp.floor((column + 0.5) * (1.0 / cols_north))
    north = column - east * cols_north + (tile_north * cols_north).astype(F32) + 0.5
    east = east + (tile_east * cols_east).astype(F32) + 0.5
    numer = jnp.sum(weight * values * values, axis=1, keepdims=True)
    variance = jnp.sum(spread * spread, axis=0, keepdims=True)
    denom = jnp.sum(weight * variance, axis=1, keepdims=True) / (members - 1)
    out_ref[0:members, :] = spread * root
    row = lax.broadcasted_iota(jnp.int32, (ROWS - members, slots), 0)
    rest = jnp.zeros((ROWS - members, slots), F32)
    for place, value in enumerate((values * root, east, north, numer, denom)):
        rest = jnp.where(row == place, value, rest)
    out_ref[members:ROWS, :] = rest


def gram_kernel(members, cols_east, cols_north, obs_refs, out_ref, lhs_hi, lhs_lo, rhs_hi, rhs_lo):
    each = obs_refs[0].shape[0] // ROWS
    tiles = each * len(obs_refs)
    slots = obs_refs[0].shape[1]
    offsets, pull_row, total = pair_rows(members)
    regions_north = cols_north // SPAN
    deep = regions_north // 2 + 2
    lanes = 2 * LANES
    tile_east, tile_north = lax.axis_index("gx"), lax.axis_index("gy")
    count_north = lax.axis_size("gy")
    lane = lax.broadcasted_iota(jnp.int32, (1, lanes), 1)
    half = (lane >= LANES).astype(jnp.int32)
    inner = (lane - half * LANES).astype(F32)
    place_east = jnp.floor((inner + 0.5) / deep)
    place_north = inner - place_east * deep
    centre_east = (tile_east * cols_east).astype(F32) + (place_east - 1.0) * SPAN + 0.5 * SPAN
    place_north = place_north + (tile_north * regions_north + half * (regions_north // 2) - 1).astype(F32)
    place_north = jnp.clip(place_north, 0.0, float(count_north * regions_north - 1))
    centre_north = place_north * SPAN + 0.5 * SPAN
    period = float(lax.axis_size("gx") * cols_east)
    radius = float(cols_east)
    inv_radius = 1.0 / radius
    centre_north = centre_north * inv_radius

    def build(t):
        obs_ref, base = obs_refs[t // each], t % each * ROWS
        place = jnp.transpose(obs_ref[base + members : base + ROWS, :])
        east, north = place[:, 1:2], place[:, 2:3] * inv_radius
        away = jnp.abs(east - centre_east)
        away = jnp.minimum(away, period - away) * inv_radius
        up = north - centre_north
        near = jnp.maximum(1.0 - away * away - up * up, 0.0)
        taper = near * near
        span = slice(t * slots, (t + 1) * slots)
        hi = taper.astype(BF16)
        rhs_hi[span, :] = hi
        rhs_lo[span, :] = (taper - hi.astype(F32)).astype(BF16)
        for i in range(0, members, 2):
            first = (i // SUB) * SUB
            rows = obs_ref[base + first : base + members, :]
            table = jnp.concatenate(
                [obs_ref[base + i : base + i + 1, :] * rows, obs_ref[base + i + 1 : base + i + 2, :] * rows], axis=0
            )
            hi = table.astype(BF16)
            lhs_hi[offsets[i] : offsets[i] + table.shape[0], span] = hi
            lhs_lo[offsets[i] : offsets[i] + table.shape[0], span] = (table - hi.astype(F32)).astype(BF16)
        table = obs_ref[base + members : base + members + 1, :] * obs_ref[base : base + members, :]
        table = jnp.concatenate([table, jnp.zeros((total - pull_row - members, slots), F32)], axis=0)
        hi = table.astype(BF16)
        lhs_hi[pull_row:total, span] = hi
        lhs_lo[pull_row:total, span] = (table - hi.astype(F32)).astype(BF16)

    def multiply(start, stop):
        span = slice(start * slots, stop * slots)
        left = jnp.concatenate([lhs_hi[:, span], lhs_lo[:, span], lhs_hi[:, span]], axis=1)
        right = jnp.concatenate([rhs_hi[span, :], rhs_hi[span, :], rhs_lo[span, :]], axis=0)
        return jnp.dot(left, right, preferred_element_type=F32)

    edges = [0, *range(1, tiles, 2), tiles]
    parts = list(zip(edges, edges[1:]))
    build(0)
    for n, (start, stop) in enumerate(parts):
        if n + 1 < len(parts):
            for t in range(*parts[n + 1]):
                build(t)
        if n == 0:
            out_ref[...] = multiply(start, stop)
        else:
            out_ref[...] += multiply(start, stop)


def gram_table(*bundles, members, cols_east, cols_north):
    total = pair_rows(members)[2]
    deep = sum(x.shape[0] // ROWS * x.shape[1] for x in bundles)
    count = len(bundles)

    def body(*refs):
        gram_kernel(members, cols_east, cols_north, refs[:count], *refs[count:])

    return pl.pallas_call(
        body,
        out_shape=jax.ShapeDtypeStruct((total, 2 * LANES), F32),
        in_specs=[pl.BlockSpec(memory_space=pltpu.VMEM)] * count,
        out_specs=pl.BlockSpec(memory_space=pltpu.VMEM),
        scratch_shapes=[
            pltpu.VMEM((total, deep), BF16),
            pltpu.VMEM((total, deep), BF16),
            pltpu.VMEM((deep, 2 * LANES), BF16),
            pltpu.VMEM((deep, 2 * LANES), BF16),
        ],
        compiler_params=pltpu.CompilerParams(vmem_limit_bytes=(12 << 20) * count),
        cost_estimate=pl.CostEstimate(flops=6 * total * deep * 2 * LANES, bytes_accessed=1 << 21, transcendentals=0),
        name="gram_table",
    )(*bundles)


def columns_kernel(state_ref, out_ref, state_v, even_ref, odd_ref, in_sem):
    members, cols_east, cols_north, levels = state_v.shape
    pitch = even_ref.shape[0] // members

    def fetch(a):
        return pltpu.make_async_copy(state_ref.at[:, a], state_v.at[:, a], in_sem.at[a])

    for a in range(cols_east):
        fetch(a).start()
    gap = jnp.zeros((ROWS - members, levels), BF16)

    def load(a, ref):
        fetch(a).wait()
        for j in range(members):
            ref[j * pitch : j * pitch + cols_north, :] = state_v[j, a].astype(F32)

    def store(a, ref):
        for b in range(cols_north):
            column = ref[pl.ds(b, members, stride=pitch), :].astype(BF16)
            out_ref[a, b] = jnp.concatenate([column, gap], axis=0)

    def pair(t, carry):
        load(2 * t, even_ref)
        load(2 * t + 1, odd_ref)
        store(2 * t, even_ref)
        store(2 * t + 1, odd_ref)
        return carry

    lax.fori_loop(0, cols_east // 2, pair, 0)


def by_column(background):
    members, cols_east, cols_north, levels = background.shape
    shape = (cols_east, cols_north, ROWS, levels)
    return pl.pallas_call(
        columns_kernel,
        out_shape=jax.ShapeDtypeStruct(shape, BF16),
        in_specs=[pl.BlockSpec(memory_space=pltpu.HBM)],
        out_specs=pl.BlockSpec(memory_space=pltpu.VMEM),
        scratch_shapes=[
            pltpu.VMEM(background.shape, BF16),
            pltpu.VMEM((members * (cols_north + 1), levels), F32),
            pltpu.VMEM((members * (cols_north + 1), levels), F32),
            pltpu.SemaphoreType.DMA((cols_east,)),
        ],
        compiler_params=pltpu.CompilerParams(vmem_limit_bytes=20 << 20),
        cost_estimate=pl.CostEstimate(flops=0, bytes_accessed=12 << 20, transcendentals=0),
        name="columns",
    )(pltpu.with_memory_space_constraint(background, pltpu.HBM))


def analysis_kernel(
    members, grams, sums, column_ref, out_ref, u_ref, v_ref, t_ref, s_ref, m_ref, w_ref, mean_ref, l_ref, o_refs, out_v, out_sem
):
    _, cols_east, cols_north, levels = out_v.shape
    offsets, pull_row, _ = pair_rows(members)
    wide = 2 * LANES
    blocks = members // SUB
    pitch = cols_east * cols_north + 1
    half_cols = cols_north // 2
    half = cols_east * half_cols
    deep = half_cols // SPAN + 2

    def flush(a):
        return pltpu.make_async_copy(out_v.at[:, a], out_ref.at[:, a], out_sem.at[a])

    row = lax.broadcasted_iota(jnp.int32, (half, LANES), 0).astype(F32)
    lane = lax.broadcasted_iota(jnp.int32, (half, LANES), 1).astype(F32)
    col_east = jnp.floor((row + 0.5) / half_cols)
    col_north = row - col_east * half_cols
    reg_east = jnp.floor((lane + 0.5) / deep)
    reg_north = lane - reg_east * deep
    hat_east = jnp.maximum(1.0 - jnp.abs(col_east + 0.5 - ((reg_east - 1.0) * SPAN + 0.5 * SPAN)) / SPAN, 0.0)
    hat_north = jnp.maximum(1.0 - jnp.abs(col_north + 0.5 - ((reg_north - 1.0) * SPAN + 0.5 * SPAN)) / SPAN, 0.0)
    hats = (hat_east * hat_north).astype(BF16)
    w_ref[:, 0:LANES] = hats
    w_ref[:, LANES:wide] = hats

    total = functools.reduce(lambda x, y: x + y, [x[...] for x in sums])
    prior = (members - 1) / (total[0:1, 0:1] / total[1:2, 0:1])
    sub = lax.broadcasted_iota(jnp.int32, (SUB, wide), 0)
    gap = jnp.zeros((SLOT - ROWS, wide), BF16)
    fold = -(-members // (2 * SUB)) * SUB

    def gram(row0):
        return functools.reduce(lambda x, y: x + y, [g[row0 : row0 + SUB, :] for g in grams])

    def part(h, k):
        return t_ref[h, k * ROWS : (k + 1) * ROWS, :]

    def put(k, blocks_k):
        table = jnp.concatenate(blocks_k + [jnp.zeros((ROWS - members, wide), F32)], axis=0)
        hi = table.astype(BF16)
        lo = (table - hi.astype(F32)).astype(BF16)
        for h in range(2):
            t_ref[h, k * ROWS : (k + 1) * ROWS, 0:LANES] = hi[:, h * LANES : (h + 1) * LANES]
            t_ref[h, k * ROWS : (k + 1) * ROWS, LANES:wide] = lo[:, h * LANES : (h + 1) * LANES]

    def spread(h, right):
        return lax.dot_general(w_ref[...], right, (((1,), (1,)), ((), ())), preferred_element_type=F32)

    scale = math.sqrt(members - 1)
    mean_ref[...] = jnp.zeros_like(mean_ref)

    def factor_rows(start, stop):
        for i in range(start, stop):
            own = i // SUB
            acc_u = [gram(offsets[i] + SUB * b) for b in range(blocks - own)]
            at = sub == i % SUB
            acc_u[0] = acc_u[0] + jnp.where(at, prior, 0.0)
            acc_v = [jnp.zeros((SUB, wide), F32) for _ in range(own)] + [jnp.where(at, scale, 0.0)]
            for p in range(i):
                row = p * members
                factor = u_ref[row + i : row + i + 1, :]
                for b in range(own, blocks):
                    acc_u[b - own] = acc_u[b - own] - factor * u_ref[row + SUB * b : row + SUB * (b + 1), :]
                for b in range(p // SUB + 1):
                    acc_v[b] = acc_v[b] - factor * v_ref[row + SUB * b : row + SUB * (b + 1), :]
            inv = lax.rsqrt(acc_u[0][i % SUB : i % SUB + 1, :])
            for b in range(own, blocks):
                u_ref[i * members + SUB * b : i * members + SUB * (b + 1), :] = acc_u[b - own] * inv
            for b in range(own + 1):
                v_ref[i * members + SUB * b : i * members + SUB * (b + 1), :] = acc_v[b] * inv

    def put_rows(start, stop):
        most = (stop - 1) // SUB + 1
        pulls = [gram(pull_row + SUB * b) * (1.0 / (members - 1)) for b in range(most)]
        mean_w = [mean_ref[SUB * b : SUB * (b + 1), :] for b in range(most)]
        for i in range(start, stop):
            count = i // SUB + 1
            rows = [v_ref[i * members + SUB * b : i * members + SUB * (b + 1), :] for b in range(count)]
            solved = functools.reduce(lambda x, y: x + y, [x * y for x, y in zip(rows, pulls)])
            solved = jnp.sum(solved, axis=0, keepdims=True)
            shift = jnp.sum(functools.reduce(lambda x, y: x + y, rows), axis=0, keepdims=True) * (-1.0 / members)
            for b in range(count):
                mean_w[b] = mean_w[b] + solved * rows[b]
            rows = [x + shift for x in rows]
            put(i, rows + [jnp.broadcast_to(shift, (SUB, wide))] * (blocks - count))
        for b in range(most):
            mean_ref[SUB * b : SUB * (b + 1), :] = mean_w[b]

    def spread_rows(k):
        for h in range(2):
            sides = []
            for n in (k, k + 1):
                other = part(h, n + fold) if n + fold < members else jnp.zeros((ROWS, wide), BF16)
                sides += [part(h, n), gap, other, gap]
            both = spread(h, jnp.concatenate(sides, axis=0))
            s_ref[k * pitch + h * half : k * pitch + (h + 1) * half, :] = both[:, 0:LANES]
            s_ref[(k + 1) * pitch + h * half : (k + 1) * pitch + (h + 1) * half, :] = both[:, LANES:wide]

    def spread_mean():
        mean_w = [mean_ref[SUB * b : SUB * (b + 1), :] for b in range(blocks)]
        mean_sum = jnp.sum(functools.reduce(lambda x, y: x + y, mean_w), axis=0, keepdims=True)
        shift = (1.0 - mean_sum) * (1.0 / members)
        put(members, [x + shift for x in mean_w])
        for h in range(2):
            right = jnp.concatenate([part(h, members), gap, part(h, members), gap], axis=0)
            m_ref[h * half : (h + 1) * half, :] = spread(h, right)

    for i in range(members):
        factor_rows(i, i + 1)
        put_rows(i, i + 1)
        if i % 2 and i >= fold:
            spread_rows(i - fold - 1)
    for k in range(members - fold, fold, 2):
        spread_rows(k)
    spread_mean()
    lower_lane = lax.broadcasted_iota(jnp.int32, (fold, LANES), 1) < SLOT
    blank = jnp.zeros((SLOT - ROWS, 2 * levels), BF16)
    pitch_o = members + 1

    def matrix(a, b):
        h, within = b // half_cols, b % half_cols
        place = h * half + a * half_cols + within
        value = s_ref[pl.ds(place, fold, stride=pitch), :] + m_ref[pl.ds(place, 1), :]
        high = value.astype(BF16).astype(F32)
        low = value - high
        turned = pltpu.roll(jnp.where(lower_lane, low, high), SLOT, 1)
        first = jnp.where(lower_lane, high, turned)
        second = jnp.where(lower_lane, turned, low)
        return [first, second[0 : members - fold, :]]

    def prepare(a, b, slot):
        left = jnp.concatenate(matrix(a, b) + matrix(a, b + 1), axis=0).astype(BF16)
        l_ref[slot, b // 2] = left

    def apply(a, b, slot, o_ref):
        right = jnp.concatenate([column_ref[a, b], column_ref[a, b + 1]], axis=1)
        right = jnp.concatenate([right, blank, right, blank], axis=0)
        both = jnp.dot(l_ref[slot, b // 2], right, preferred_element_type=F32)
        o_ref[b * pitch_o : b * pitch_o + members, :] = both[:members, 0:levels]
        o_ref[(b + 1) * pitch_o : (b + 1) * pitch_o + members, :] = both[members:, levels:]

    def emit(a, k, o_ref):
        out_v[k, a] = o_ref[pl.ds(k, cols_north, stride=pitch_o), :].astype(BF16)

    group = 4

    def column_rows(t, carry):
        for s in range(group):
            a = group * t + s
            done = 0
            for b in range(0, cols_north, 2):
                apply(a, b, s % 2, o_refs[s % 2])
                prepare(jnp.minimum(a + 1, cols_east - 1), b, (s + 1) % 2)
                upto = members * (b + 2) // cols_north
                if s:
                    for k in range(done, upto):
                        emit(a - 1, k, o_refs[(s - 1) % 2])
                done = upto
            if s:
                flush(a - 1).start()
        a = group * t + group - 1
        for k in range(members):
            emit(a, k, o_refs[(group - 1) % 2])
        flush(a).start()
        return carry

    for b in range(0, cols_north, 2):
        prepare(0, b, 0)
    lax.fori_loop(0, cols_east // group, column_rows, 0)
    for a in range(cols_east):
        flush(a).wait()


def analyse(grams, sums, columns, members):
    cols_east, cols_north, _, levels = columns.shape
    count = cols_east * cols_north
    tables, most = len(grams), len(grams) + len(sums)

    def body(*refs):
        rest = refs[most:]
        analysis_kernel(members, refs[:tables], refs[tables:most], *rest[:10], rest[10:12], *rest[12:])

    vmem = pl.BlockSpec(memory_space=pltpu.VMEM)
    hbm = pl.BlockSpec(memory_space=pltpu.HBM)
    pitch = count + 1
    shape = (members, cols_east, cols_north, levels)
    return pl.pallas_call(
        body,
        out_shape=jax.ShapeDtypeStruct(shape, BF16),
        in_specs=[vmem] * (most + 1),
        out_specs=hbm,
        scratch_shapes=[
            pltpu.VMEM((members * members, 2 * LANES), F32),
            pltpu.VMEM((members * members, 2 * LANES), F32),
            pltpu.VMEM((2, (members + 1) * ROWS, 2 * LANES), BF16),
            pltpu.VMEM((-(-members // (2 * SUB)) * SUB * pitch, LANES), F32),
            pltpu.VMEM((count, LANES), F32),
            pltpu.VMEM((count // 2, 2 * LANES), BF16),
            pltpu.VMEM((members, 2 * LANES), F32),
            pltpu.VMEM((2, cols_north // 2, 2 * members, LANES), BF16),
            pltpu.VMEM((cols_north * (members + 1), levels), F32),
            pltpu.VMEM((cols_north * (members + 1), levels), F32),
            pltpu.VMEM(shape, BF16),
            pltpu.SemaphoreType.DMA((cols_east,)),
        ],
        compiler_params=pltpu.CompilerParams(vmem_limit_bytes=30 << 20),
        name="analyse",
    )(*grams, *sums, columns)


def rotate(value, axis, step):
    count = lax.axis_size(axis)
    return lax.ppermute(value, axis, [(i, (i + step) % count) for i in range(count)])


def swap(value, axis, bits):
    count = lax.axis_size(axis)
    return lax.ppermute(value, axis, [(i, i ^ bits) for i in range(count) if i ^ bits < count])


def swap_beside(value, axis):
    count = lax.axis_size(axis)
    pairs = [(i, ((i + 1) ^ 1) - 1) for i in range(count)]
    return lax.ppermute(value, axis, [(i, j) for i, j in pairs if 0 <= j < count])


def per_device(background, obs_perturb, innovation, obs_precision, obs_column, obs_count):
    members, cols_east, cols_north, levels = background.shape
    slots = obs_perturb.shape[3]
    count_east, count_north = lax.axis_size("gx"), lax.axis_size("gy")
    vmem = pl.BlockSpec(memory_space=pltpu.VMEM)
    hbm = pl.BlockSpec(memory_space=pltpu.HBM)
    inputs = (obs_perturb[0, 0], innovation[0], obs_precision[0], obs_column[0])
    bundle = pl.pallas_call(
        functools.partial(prep_kernel, cols_east, cols_north),
        out_shape=jax.ShapeDtypeStruct((ROWS, slots), F32),
        in_specs=[pl.BlockSpec(memory_space=pltpu.SMEM)] + [hbm] * 4,
        out_specs=vmem,
        scratch_shapes=[pltpu.VMEM(x.shape, x.dtype) for x in inputs] + [pltpu.SemaphoreType.DMA((4,))],
        compiler_params=pltpu.CompilerParams(vmem_limit_bytes=2 << 20),
        name="prep",
    )(obs_count, *(pltpu.with_memory_space_constraint(x, pltpu.HBM) for x in inputs))
    steps = sorted({s % count_east for s in (-2, -1, 1, 2)} - {0})
    if count_east == 4:
        around = [swap(bundle, "gx", bits) for bits in (1, 2, 3)]
    else:
        around = [rotate(bundle, "gx", s) for s in steps]
    *around, columns = lax.optimization_barrier((*around, by_column(background)))
    own = jnp.concatenate([bundle] + around, axis=0)
    beside = swap_beside(own, "gy")
    partner = swap(own, "gy", 1)

    def row_sum(bundles):
        each = bundles.reshape(-1, ROWS, slots)[:, members + 3 : members + 5, 0:LANES]
        return jnp.sum(each, axis=0)

    table = functools.partial(gram_table, members=members, cols_east=cols_east, cols_north=cols_north)
    if len(steps) + 1 == count_east and count_north == 8:
        pair = row_sum(own) + row_sum(partner)
        own, pair = lax.optimization_barrier((own, pair))
        sums = [pair] + [swap(pair, "gy", bits) for bits in (2, 4, 6)]
    else:
        sums = [lax.psum(bundle[members + 3 : members + 5, 0:LANES], ("gx", "gy"))]
    grams = [table(own), table(partner, beside)]
    return analyse(grams, sums, columns, members)


def solution(mesh):
    return jax.shard_map(
        per_device,
        mesh=mesh,
        in_specs=(
            P(None, "gx", "gy", None),
            P("gx", "gy", None, None),
            P("gx", "gy", None),
            P("gx", "gy", None),
            P("gx", "gy", None),
            P("gx", "gy"),
        ),
        out_specs=P(None, "gx", "gy", None),
        check_vma=False,
    )
```

```python
import functools
import math

import jax
import jax.numpy as jnp
from jax import lax
from jax.experimental import pallas as pl
from jax.experimental.pallas import tpu as pltpu
from jax.sharding import PartitionSpec as P

SPAN = 2
LANES = 128
SUB = 8
ROWS = 48
SLOT = 64
F32 = jnp.float32
BF16 = jnp.bfloat16


def pair_rows(members):
    offsets, total = [], 0
    for i in range(members):
        offsets.append(total)
        total += members - (i // SUB) * SUB
    pull = total
    total += members
    return offsets, pull, -(-total // 16) * 16


def prep_kernel(
    cols_east, cols_north, count_ref, perturb_hbm, innov_hbm, prec_hbm, column_hbm, out_ref,
    perturb_ref, innov_ref, prec_ref, column_ref, sem,
):
    pairs = ((perturb_hbm, perturb_ref), (innov_hbm, innov_ref), (prec_hbm, prec_ref), (column_hbm, column_ref))
    copies = [pltpu.make_async_copy(src, dst, sem.at[n]) for n, (src, dst) in enumerate(pairs)]
    for copy in copies:
        copy.start()
    for copy in copies:
        copy.wait()
    members, slots = perturb_ref.shape
    tile_east, tile_north = lax.axis_index("gx"), lax.axis_index("gy")
    values, column = innov_ref[...], column_ref[...].astype(F32)
    spread = perturb_ref[...].astype(F32)
    spread = spread - jnp.sum(spread, axis=0, keepdims=True) / members
    lane = lax.broadcasted_iota(jnp.int32, (1, slots), 1)
    weight = jnp.where(lane < count_ref[0, 0], prec_ref[...], 0.0)
    root = jnp.sqrt(weight)
    east = jnp.floor((column + 0.5) * (1.0 / cols_north))
    north = column - east * cols_north + (tile_north * cols_north).astype(F32) + 0.5
    east = east + (tile_east * cols_east).astype(F32) + 0.5
    numer = jnp.sum(weight * values * values, axis=1, keepdims=True)
    variance = jnp.sum(spread * spread, axis=0, keepdims=True)
    denom = jnp.sum(weight * variance, axis=1, keepdims=True) / (members - 1)
    out_ref[0:members, :] = spread * root
    row = lax.broadcasted_iota(jnp.int32, (ROWS - members, slots), 0)
    rest = jnp.zeros((ROWS - members, slots), F32)
    for place, value in enumerate((values * root, east, north, numer, denom)):
        rest = jnp.where(row == place, value, rest)
    out_ref[members:ROWS, :] = rest


def gram_kernel(members, cols_east, cols_north, obs_refs, out_ref, lhs_hi, lhs_lo, rhs_hi, rhs_lo):
    each = obs_refs[0].shape[0] // ROWS
    tiles = each * len(obs_refs)
    slots = obs_refs[0].shape[1]
    offsets, pull_row, total = pair_rows(members)
    regions_north = cols_north // SPAN
    deep = regions_north // 2 + 2
    lanes = 2 * LANES
    tile_east, tile_north = lax.axis_index("gx"), lax.axis_index("gy")
    count_north = lax.axis_size("gy")
    lane = lax.broadcasted_iota(jnp.int32, (1, lanes), 1)
    half = (lane >= LANES).astype(jnp.int32)
    inner = (lane - half * LANES).astype(F32)
    place_east = jnp.floor((inner + 0.5) / deep)
    place_north = inner - place_east * deep
    centre_east = (tile_east * cols_east).astype(F32) + (place_east - 1.0) * SPAN + 0.5 * SPAN
    place_north = place_north + (tile_north * regions_north + half * (regions_north // 2) - 1).astype(F32)
    place_north = jnp.clip(place_north, 0.0, float(count_north * regions_north - 1))
    centre_north = place_north * SPAN + 0.5 * SPAN
    period = float(lax.axis_size("gx") * cols_east)
    radius = float(cols_east)
    inv_radius = 1.0 / radius
    centre_north = centre_north * inv_radius

    def build(t):
        obs_ref, base = obs_refs[t // each], t % each * ROWS
        place = jnp.transpose(obs_ref[base + members : base + ROWS, :])
        east, north = place[:, 1:2], place[:, 2:3] * inv_radius
        away = jnp.abs(east - centre_east)
        away = jnp.minimum(away, period - away) * inv_radius
        up = north - centre_north
        near = jnp.maximum(1.0 - away * away - up * up, 0.0)
        taper = near * near
        span = slice(t * slots, (t + 1) * slots)
        hi = taper.astype(BF16)
        rhs_hi[span, :] = hi
        rhs_lo[span, :] = (taper - hi.astype(F32)).astype(BF16)
        for i in range(0, members, 2):
            first = (i // SUB) * SUB
            rows = obs_ref[base + first : base + members, :]
            table = jnp.concatenate(
                [obs_ref[base + i : base + i + 1, :] * rows, obs_ref[base + i + 1 : base + i + 2, :] * rows], axis=0
            )
            hi = table.astype(BF16)
            lhs_hi[offsets[i] : offsets[i] + table.shape[0], span] = hi
            lhs_lo[offsets[i] : offsets[i] + table.shape[0], span] = (table - hi.astype(F32)).astype(BF16)
        table = obs_ref[base + members : base + members + 1, :] * obs_ref[base : base + members, :]
        table = jnp.concatenate([table, jnp.zeros((total - pull_row - members, slots), F32)], axis=0)
        hi = table.astype(BF16)
        lhs_hi[pull_row:total, span] = hi
        lhs_lo[pull_row:total, span] = (table - hi.astype(F32)).astype(BF16)

    def multiply(start, stop):
        span = slice(start * slots, stop * slots)
        left = jnp.concatenate([lhs_hi[:, span], lhs_lo[:, span], lhs_hi[:, span]], axis=1)
        right = jnp.concatenate([rhs_hi[span, :], rhs_hi[span, :], rhs_lo[span, :]], axis=0)
        return jnp.dot(left, right, preferred_element_type=F32)

    edges = [0, *range(1, tiles, 2 if tiles > each else 3), tiles]
    parts = list(zip(edges, edges[1:]))
    build(0)
    for n, (start, stop) in enumerate(parts):
        if n + 1 < len(parts):
            for t in range(*parts[n + 1]):
                build(t)
        if n == 0:
            out_ref[...] = multiply(start, stop)
        else:
            out_ref[...] += multiply(start, stop)


def gram_table(*bundles, members, cols_east, cols_north):
    total = pair_rows(members)[2]
    deep = sum(x.shape[0] // ROWS * x.shape[1] for x in bundles)
    count = len(bundles)

    def body(*refs):
        gram_kernel(members, cols_east, cols_north, refs[:count], *refs[count:])

    return pl.pallas_call(
        body,
        out_shape=jax.ShapeDtypeStruct((total, 2 * LANES), F32),
        in_specs=[pl.BlockSpec(memory_space=pltpu.VMEM)] * count,
        out_specs=pl.BlockSpec(memory_space=pltpu.VMEM),
        scratch_shapes=[
            pltpu.VMEM((total, deep), BF16),
            pltpu.VMEM((total, deep), BF16),
            pltpu.VMEM((deep, 2 * LANES), BF16),
            pltpu.VMEM((deep, 2 * LANES), BF16),
        ],
        compiler_params=pltpu.CompilerParams(vmem_limit_bytes=(12 << 20) * count),
        cost_estimate=pl.CostEstimate(flops=6 * total * deep * 2 * LANES, bytes_accessed=1 << 21, transcendentals=0),
        name="gram_table",
    )(*bundles)


def columns_kernel(state_ref, out_ref, state_v, even_ref, odd_ref, in_sem):
    members, cols_east, cols_north, levels = state_v.shape
    pitch = even_ref.shape[0] // members

    def fetch(a):
        return pltpu.make_async_copy(state_ref.at[:, a], state_v.at[:, a], in_sem.at[a])

    for a in range(cols_east):
        fetch(a).start()
    gap = jnp.zeros((ROWS - members, levels), BF16)

    def load(a, ref):
        fetch(a).wait()
        for j in range(members):
            ref[j * pitch : j * pitch + cols_north, :] = state_v[j, a].astype(F32)

    def store(a, ref):
        for b in range(cols_north):
            column = ref[pl.ds(b, members, stride=pitch), :].astype(BF16)
            out_ref[a, b] = jnp.concatenate([column, gap], axis=0)

    def pair(t, carry):
        load(2 * t, even_ref)
        load(2 * t + 1, odd_ref)
        store(2 * t, even_ref)
        store(2 * t + 1, odd_ref)
        return carry

    lax.fori_loop(0, cols_east // 2, pair, 0)


def by_column(background):
    members, cols_east, cols_north, levels = background.shape
    shape = (cols_east, cols_north, ROWS, levels)
    return pl.pallas_call(
        columns_kernel,
        out_shape=jax.ShapeDtypeStruct(shape, BF16),
        in_specs=[pl.BlockSpec(memory_space=pltpu.HBM)],
        out_specs=pl.BlockSpec(memory_space=pltpu.VMEM),
        scratch_shapes=[
            pltpu.VMEM(background.shape, BF16),
            pltpu.VMEM((members * (cols_north + 1), levels), F32),
            pltpu.VMEM((members * (cols_north + 1), levels), F32),
            pltpu.SemaphoreType.DMA((cols_east,)),
        ],
        compiler_params=pltpu.CompilerParams(vmem_limit_bytes=20 << 20),
        cost_estimate=pl.CostEstimate(flops=0, bytes_accessed=12 << 20, transcendentals=0),
        name="columns",
    )(pltpu.with_memory_space_constraint(background, pltpu.HBM))


def analysis_kernel(
    members, grams, sums, column_ref, out_ref, u_ref, v_ref, t_ref, s_ref, m_ref, w_ref, mean_ref, l_ref, o_refs, out_v, out_sem
):
    _, cols_east, cols_north, levels = out_v.shape
    offsets, pull_row, _ = pair_rows(members)
    wide = 2 * LANES
    blocks = members // SUB
    pitch = cols_east * cols_north + 1
    half_cols = cols_north // 2
    half = cols_east * half_cols
    deep = half_cols // SPAN + 2

    def flush(a):
        return pltpu.make_async_copy(out_v.at[:, a], out_ref.at[:, a], out_sem.at[a])

    row = lax.broadcasted_iota(jnp.int32, (half, LANES), 0).astype(F32)
    lane = lax.broadcasted_iota(jnp.int32, (half, LANES), 1).astype(F32)
    col_east = jnp.floor((row + 0.5) / half_cols)
    col_north = row - col_east * half_cols
    reg_east = jnp.floor((lane + 0.5) / deep)
    reg_north = lane - reg_east * deep
    hat_east = jnp.maximum(1.0 - jnp.abs(col_east + 0.5 - ((reg_east - 1.0) * SPAN + 0.5 * SPAN)) / SPAN, 0.0)
    hat_north = jnp.maximum(1.0 - jnp.abs(col_north + 0.5 - ((reg_north - 1.0) * SPAN + 0.5 * SPAN)) / SPAN, 0.0)
    hats = (hat_east * hat_north).astype(BF16)
    w_ref[:, 0:LANES] = hats
    w_ref[:, LANES:wide] = hats

    total = functools.reduce(lambda x, y: x + y, [x[...] for x in sums])
    prior = (members - 1) / (total[0:1, 0:1] / total[1:2, 0:1])
    sub = lax.broadcasted_iota(jnp.int32, (SUB, wide), 0)
    gap = jnp.zeros((SLOT - ROWS, wide), BF16)
    fold = -(-members // (2 * SUB)) * SUB

    def gram(row0):
        return functools.reduce(lambda x, y: x + y, [g[row0 : row0 + SUB, :] for g in grams])

    def part(h, k):
        return t_ref[h, k * ROWS : (k + 1) * ROWS, :]

    def put(k, blocks_k):
        table = jnp.concatenate(blocks_k + [jnp.zeros((ROWS - members, wide), F32)], axis=0)
        hi = table.astype(BF16)
        lo = (table - hi.astype(F32)).astype(BF16)
        for h in range(2):
            t_ref[h, k * ROWS : (k + 1) * ROWS, 0:LANES] = hi[:, h * LANES : (h + 1) * LANES]
            t_ref[h, k * ROWS : (k + 1) * ROWS, LANES:wide] = lo[:, h * LANES : (h + 1) * LANES]

    def spread(h, right):
        return lax.dot_general(w_ref[...], right, (((1,), (1,)), ((), ())), preferred_element_type=F32)

    scale = math.sqrt(members - 1)
    mean_ref[...] = jnp.zeros_like(mean_ref)

    def factor_rows(start, stop):
        for i in range(start, stop):
            own = i // SUB
            acc_u = [gram(offsets[i] + SUB * b) for b in range(blocks - own)]
            at = sub == i % SUB
            acc_u[0] = acc_u[0] + jnp.where(at, prior, 0.0)
            acc_v = [jnp.zeros((SUB, wide), F32) for _ in range(own)] + [jnp.where(at, scale, 0.0)]
            for p in range(i):
                row = p * members
                factor = u_ref[row + i : row + i + 1, :]
                for b in range(own, blocks):
                    acc_u[b - own] = acc_u[b - own] - factor * u_ref[row + SUB * b : row + SUB * (b + 1), :]
                for b in range(p // SUB + 1):
                    acc_v[b] = acc_v[b] - factor * v_ref[row + SUB * b : row + SUB * (b + 1), :]
            inv = lax.rsqrt(acc_u[0][i % SUB : i % SUB + 1, :])
            for b in range(own, blocks):
                u_ref[i * members + SUB * b : i * members + SUB * (b + 1), :] = acc_u[b - own] * inv
            for b in range(own + 1):
                v_ref[i * members + SUB * b : i * members + SUB * (b + 1), :] = acc_v[b] * inv

    def put_rows(start, stop):
        most = (stop - 1) // SUB + 1
        pulls = [gram(pull_row + SUB * b) * (1.0 / (members - 1)) for b in range(most)]
        mean_w = [mean_ref[SUB * b : SUB * (b + 1), :] for b in range(most)]
        for i in range(start, stop):
            count = i // SUB + 1
            rows = [v_ref[i * members + SUB * b : i * members + SUB * (b + 1), :] for b in range(count)]
            solved = functools.reduce(lambda x, y: x + y, [x * y for x, y in zip(rows, pulls)])
            solved = jnp.sum(solved, axis=0, keepdims=True)
            shift = jnp.sum(functools.reduce(lambda x, y: x + y, rows), axis=0, keepdims=True) * (-1.0 / members)
            for b in range(count):
                mean_w[b] = mean_w[b] + solved * rows[b]
            rows = [x + shift for x in rows]
            put(i, rows + [jnp.broadcast_to(shift, (SUB, wide))] * (blocks - count))
        for b in range(most):
            mean_ref[SUB * b : SUB * (b + 1), :] = mean_w[b]

    def spread_rows(k):
        for h in range(2):
            sides = []
            for n in (k, k + 1):
                other = part(h, n + fold) if n + fold < members else jnp.zeros((ROWS, wide), BF16)
                sides += [part(h, n), gap, other, gap]
            both = spread(h, jnp.concatenate(sides, axis=0))
            s_ref[k * pitch + h * half : k * pitch + (h + 1) * half, :] = both[:, 0:LANES]
            s_ref[(k + 1) * pitch + h * half : (k + 1) * pitch + (h + 1) * half, :] = both[:, LANES:wide]

    def spread_mean():
        mean_w = [mean_ref[SUB * b : SUB * (b + 1), :] for b in range(blocks)]
        mean_sum = jnp.sum(functools.reduce(lambda x, y: x + y, mean_w), axis=0, keepdims=True)
        shift = (1.0 - mean_sum) * (1.0 / members)
        put(members, [x + shift for x in mean_w])
        for h in range(2):
            right = jnp.concatenate([part(h, members), gap, part(h, members), gap], axis=0)
            m_ref[h * half : (h + 1) * half, :] = spread(h, right)

    for i in range(members):
        factor_rows(i, i + 1)
        put_rows(i, i + 1)
        if i % 2 and i >= fold:
            spread_rows(i - fold - 1)
    for k in range(members - fold, fold, 2):
        spread_rows(k)
    spread_mean()
    lower_lane = lax.broadcasted_iota(jnp.int32, (fold, LANES), 1) < SLOT
    blank = jnp.zeros((SLOT - ROWS, 2 * levels), BF16)
    pitch_o = members + 1

    def matrix(a, b):
        h, within = b // half_cols, b % half_cols
        place = h * half + a * half_cols + within
        value = s_ref[pl.ds(place, fold, stride=pitch), :] + m_ref[pl.ds(place, 1), :]
        high = value.astype(BF16).astype(F32)
        low = value - high
        turned = pltpu.roll(jnp.where(lower_lane, low, high), SLOT, 1)
        first = jnp.where(lower_lane, high, turned)
        second = jnp.where(lower_lane, turned, low)
        return [first, second[0 : members - fold, :]]

    def prepare(a, b, slot):
        left = jnp.concatenate(matrix(a, b) + matrix(a, b + 1), axis=0).astype(BF16)
        l_ref[slot, b // 2] = left

    def apply(a, b, slot, o_ref):
        right = jnp.concatenate([column_ref[a, b], column_ref[a, b + 1]], axis=1)
        right = jnp.concatenate([right, blank, right, blank], axis=0)
        both = jnp.dot(l_ref[slot, b // 2], right, preferred_element_type=F32)
        o_ref[b * pitch_o : b * pitch_o + members, :] = both[:members, 0:levels]
        o_ref[(b + 1) * pitch_o : (b + 1) * pitch_o + members, :] = both[members:, levels:]

    def emit(a, k, o_ref):
        out_v[k, a] = o_ref[pl.ds(k, cols_north, stride=pitch_o), :].astype(BF16)

    group = 8

    def column_rows(t, carry):
        for s in range(group):
            a = group * t + s
            done = 0
            for b in range(0, cols_north, 2):
                apply(a, b, s % 2, o_refs[s % 2])
                prepare(jnp.minimum(a + 1, cols_east - 1), b, (s + 1) % 2)
                upto = members * (b + 2) // cols_north
                if s:
                    for k in range(done, upto):
                        emit(a - 1, k, o_refs[(s - 1) % 2])
                done = upto
            if s:
                flush(a - 1).start()
        a = group * t + group - 1
        for k in range(members):
            emit(a, k, o_refs[(group - 1) % 2])
        flush(a).start()
        return carry

    for b in range(0, cols_north, 2):
        prepare(0, b, 0)
    lax.fori_loop(0, cols_east // group, column_rows, 0)
    for a in range(cols_east):
        flush(a).wait()


def analyse(grams, sums, columns, members):
    cols_east, cols_north, _, levels = columns.shape
    count = cols_east * cols_north
    tables, most = len(grams), len(grams) + len(sums)

    def body(*refs):
        rest = refs[most:]
        analysis_kernel(members, refs[:tables], refs[tables:most], *rest[:10], rest[10:12], *rest[12:])

    vmem = pl.BlockSpec(memory_space=pltpu.VMEM)
    hbm = pl.BlockSpec(memory_space=pltpu.HBM)
    pitch = count + 1
    shape = (members, cols_east, cols_north, levels)
    return pl.pallas_call(
        body,
        out_shape=jax.ShapeDtypeStruct(shape, BF16),
        in_specs=[vmem] * (most + 1),
        out_specs=hbm,
        scratch_shapes=[
            pltpu.VMEM((members * members, 2 * LANES), F32),
            pltpu.VMEM((members * members, 2 * LANES), F32),
            pltpu.VMEM((2, (members + 1) * ROWS, 2 * LANES), BF16),
            pltpu.VMEM((-(-members // (2 * SUB)) * SUB * pitch, LANES), F32),
            pltpu.VMEM((count, LANES), F32),
            pltpu.VMEM((count // 2, 2 * LANES), BF16),
            pltpu.VMEM((members, 2 * LANES), F32),
            pltpu.VMEM((2, cols_north // 2, 2 * members, LANES), BF16),
            pltpu.VMEM((cols_north * (members + 1), levels), F32),
            pltpu.VMEM((cols_north * (members + 1), levels), F32),
            pltpu.VMEM(shape, BF16),
            pltpu.SemaphoreType.DMA((cols_east,)),
        ],
        compiler_params=pltpu.CompilerParams(vmem_limit_bytes=30 << 20),
        name="analyse",
    )(*grams, *sums, columns)


def rotate(value, axis, step):
    count = lax.axis_size(axis)
    return lax.ppermute(value, axis, [(i, (i + step) % count) for i in range(count)])


def swap(value, axis, bits):
    count = lax.axis_size(axis)
    return lax.ppermute(value, axis, [(i, i ^ bits) for i in range(count) if i ^ bits < count])


def swap_beside(value, axis):
    count = lax.axis_size(axis)
    pairs = [(i, ((i + 1) ^ 1) - 1) for i in range(count)]
    return lax.ppermute(value, axis, [(i, j) for i, j in pairs if 0 <= j < count])


def per_device(background, obs_perturb, innovation, obs_precision, obs_column, obs_count):
    members, cols_east, cols_north, levels = background.shape
    slots = obs_perturb.shape[3]
    count_east, count_north = lax.axis_size("gx"), lax.axis_size("gy")
    vmem = pl.BlockSpec(memory_space=pltpu.VMEM)
    hbm = pl.BlockSpec(memory_space=pltpu.HBM)
    inputs = (obs_perturb[0, 0], innovation[0], obs_precision[0], obs_column[0])
    bundle = pl.pallas_call(
        functools.partial(prep_kernel, cols_east, cols_north),
        out_shape=jax.ShapeDtypeStruct((ROWS, slots), F32),
        in_specs=[pl.BlockSpec(memory_space=pltpu.SMEM)] + [hbm] * 4,
        out_specs=vmem,
        scratch_shapes=[pltpu.VMEM(x.shape, x.dtype) for x in inputs] + [pltpu.SemaphoreType.DMA((4,))],
        compiler_params=pltpu.CompilerParams(vmem_limit_bytes=2 << 20),
        name="prep",
    )(obs_count, *(pltpu.with_memory_space_constraint(x, pltpu.HBM) for x in inputs))
    steps = sorted({s % count_east for s in (-2, -1, 1, 2)} - {0})
    if count_east == 4:
        around = [swap(bundle, "gx", bits) for bits in (1, 2, 3)]
    else:
        around = [rotate(bundle, "gx", s) for s in steps]
    *around, columns = lax.optimization_barrier((*around, by_column(background)))
    own = jnp.concatenate([bundle] + around, axis=0)
    beside = swap_beside(own, "gy")
    partner = swap(own, "gy", 1)

    def row_sum(bundles):
        each = bundles.reshape(-1, ROWS, slots)[:, members + 3 : members + 5, 0:LANES]
        return jnp.sum(each, axis=0)

    table = functools.partial(gram_table, members=members, cols_east=cols_east, cols_north=cols_north)
    if len(steps) + 1 == count_east and count_north == 8:
        pair = row_sum(own) + row_sum(partner)
        own, pair = lax.optimization_barrier((own, pair))
        sums = [pair] + [swap(pair, "gy", bits) for bits in (2, 4, 6)]
    else:
        sums = [lax.psum(bundle[members + 3 : members + 5, 0:LANES], ("gx", "gy"))]
    grams = [table(own), table(partner, beside)]
    return analyse(grams, sums, columns, members)


def solution(mesh):
    return jax.shard_map(
        per_device,
        mesh=mesh,
        in_specs=(
            P(None, "gx", "gy", None),
            P("gx", "gy", None, None),
            P("gx", "gy", None),
            P("gx", "gy", None),
            P("gx", "gy", None),
            P("gx", "gy"),
        ),
        out_specs=P(None, "gx", "gy", None),
        check_vma=False,
    )
```
